256 devices in a mesh: gx: 16 (over z_hi, x), gy: 16 (over y, z_lo, core).
Axes of the slice: x: 4, y: 4, z: 8 (z_hi: 4, z_lo: 2; z = z_hi * 2 + z_lo), core: 2. Of those that a mesh axis runs over, the one named last changes fastest.
Arguments:
- positions: float32 [3, 32768], P(None, ('gx', 'gy')), may hold values from -1 to 512, as said below
- features: bfloat16 [64, 32768], P(None, ('gx', 'gy')), may hold values from -6 to 6
- species: int32 [32768], P(('gx', 'gy')), may hold values from 0 to 4
- edge_list: int32 [2, 917504], P(None, ('gx', 'gy')), may hold values from 0 to 319, as said below
- edge_count: int32 [256], P(('gx', 'gy')), may hold values from 1 to 3136, as said below
- send_list_x: int32 [32768], P(('gx', 'gy')), may hold values from 0 to 127, as said below
- send_list_y: int32 [16384], P(('gx', 'gy')), may hold values from 0 to 255, as said below
- radial_in: float32 [64, 8], replicated, may hold values from -12 to 12
- radial_out: float32 [192, 64], replicated, may hold values from -0.75 to 0.75
- mix_weight: float32 [64, 192], replicated, may hold values from -0.4375 to 0.4375
- out_weight: float32 [64], replicated, may hold values from -0.75 to 0.75
- species_energy: float32 [5], replicated, may hold values from -6 to 6
Outputs:
- energies: float32 [32768], P(('gx', 'gy'))
- forces: float32 [3, 32768], P(None, ('gx', 'gy'))
The draws below stay inside these ranges and needn't reach their ends.
Inputs may be any that keep to these rules, and one draw needn't show every extreme that they name: `positions`: atoms sit on a lattice of cells with random displacements; each device holds the cells of its column in a random slot order. Each pair of lattice neighbours within 2 cells is listed at most once in all, on the device of its first atom, and only if both atoms exist; its second entry never names a copy that no device sends. `edge_list`: row 0 names own slots below 128, row 1 entries of the extended list; slots from edge_count on hold zeros. `edge_count`: every device has at most 3136 live pairs, and some device has exactly 3136 in every draw; counts differ widely between devices. `send_list_x`: each half names 64 distinct own slots. `send_list_y`: each half names 32 distinct entries among own atoms and x copies.
All inputs are finite; a program needn't handle non-finite values.
Results may differ from the reference program's by a relative error of at most 0.00055.
Values sent between devices are 32-bit elements; how exact they have to be, the bound alone decides.
A program may use at most 64 MiB of HBM per device.

```python
import math
import jax
import jax.numpy as jnp
import numpy as np
from jax import lax

CHANNELS = 64
RADIAL_BASIS = 8
RADIAL_HIDDEN = 64
SPECIES = 5
LX = 4
LY = 16
LAYERS_Z = 2
REACH = 2
ATOMS_DEV = 128
GX = 64
GY = 32
EDGES_DEV = 3584
ATOMS = 32768
N_GX = 16
N_GY = 16


lattice_step = 1.6


def half_offsets():
    rows_list = []
    for layer_step in (0, 1):
        for step_x in range(-REACH, REACH + 1):
            for step_y in range(-REACH, REACH + 1):
                if layer_step == 1 or step_x > 0 or (step_x == 0 and step_y > 0):
                    rows_list.append((step_x, step_y, layer_step))
    return np.array(rows_list, np.int32)


def extended_index(target_x, target_y, target_z, slot_of):
    clip_x = jnp.clip(target_x, 0, LX - 1)
    clip_y = jnp.clip(target_y, 0, LY - 1)
    clip_z = jnp.clip(target_z, 0, LAYERS_Z - 1)
    own_site = (clip_x * LY + clip_y) * LAYERS_Z + clip_z
    own_slot = jnp.take_along_axis(slot_of, own_site.reshape(slot_of.shape[0], -1), axis=1).reshape(own_site.shape)
    lower_x = ATOMS_DEV + ((target_x + REACH) * LY + target_y) * LAYERS_Z + target_z
    upper_x = ATOMS_DEV + GX + ((target_x - LX) * LY + target_y) * LAYERS_Z + target_z
    lower_y = ATOMS_DEV + 2 * GX + ((target_x + REACH) * REACH + target_y + REACH) * LAYERS_Z + target_z
    upper_y = ATOMS_DEV + 2 * GX + GY + ((target_x + REACH) * REACH + target_y - LY) * LAYERS_Z + target_z
    middle = jnp.where(target_x < 0, lower_x, jnp.where(target_x >= LX, upper_x, own_slot))
    return jnp.where(target_y < 0, lower_y, jnp.where(target_y >= LY, upper_y, middle)).astype(jnp.int32)


def section_index(slot_of, column, row_y, layer_index):
    inner_x = jnp.clip(column, 0, LX - 1)
    own_slot = slot_of[:, (inner_x * LY + row_y) * LAYERS_Z + layer_index]
    lower_x = ATOMS_DEV + ((column + REACH) * LY + row_y) * LAYERS_Z + layer_index
    upper_x = ATOMS_DEV + GX + ((column - LX) * LY + row_y) * LAYERS_Z + layer_index
    chosen = jnp.where(column < 0, lower_x, jnp.where(column >= LX, upper_x, 0))
    inside = (column >= 0) & (column < LX)
    return jnp.where(inside[None, :], own_slot, chosen[None, :]).astype(jnp.int32)


def lattice_tables(key):
    device_total = N_GX * N_GY
    subkeys = jax.random.split(jax.random.fold_in(key, 101), device_total)
    site_order = jax.vmap(lambda subkey: jax.random.permutation(subkey, ATOMS_DEV))(subkeys).astype(jnp.int32)
    slot_of = jnp.argsort(site_order, axis=1).astype(jnp.int32)
    device_ids = jnp.arange(device_total, dtype=jnp.int32)
    column_x = (device_ids // N_GY)[:, None, None]
    column_y = (device_ids % N_GY)[:, None, None]
    cell_x = site_order // (LY * LAYERS_Z)
    cell_y = site_order // LAYERS_Z % LY
    cell_z = site_order % LAYERS_Z
    offsets = half_offsets()
    target_x = cell_x[:, :, None] + jnp.asarray(offsets[:, 0])[None, None, :]
    target_y = cell_y[:, :, None] + jnp.asarray(offsets[:, 1])[None, None, :]
    target_z = cell_z[:, :, None] + jnp.asarray(offsets[:, 2])[None, None, :]
    global_x = column_x * LX + target_x
    global_y = column_y * LY + target_y
    inside = (target_z < LAYERS_Z) & (global_x >= 0) & (global_x < N_GX * LX) & (global_y >= 0) & (global_y < N_GY * LY)
    density = jax.random.randint(jax.random.fold_in(key, 102), (device_total,), 1, 9)
    density = density.at[N_GX // 2 * N_GY + N_GY // 2].set(8)
    coin_draw = jax.random.randint(jax.random.fold_in(key, 103), inside.shape, 0, 8)
    kept_edges = inside & (coin_draw < density[:, None, None])
    target_slot = extended_index(target_x, target_y, target_z, slot_of)
    kept_flat = kept_edges.reshape(device_total, -1)
    placed = jnp.cumsum(kept_flat.astype(jnp.int32), axis=1) - 1
    placed = jnp.where(kept_flat, placed, EDGES_DEV)
    owners = jnp.broadcast_to(jnp.arange(ATOMS_DEV, dtype=jnp.int32)[None, :, None], kept_edges.shape).reshape(device_total, -1)
    device_rows = jnp.broadcast_to(device_ids[:, None], placed.shape)
    first_end = jnp.zeros((device_total, EDGES_DEV), jnp.int32).at[device_rows, placed].set(owners, mode='drop')
    second_end = jnp.zeros((device_total, EDGES_DEV), jnp.int32).at[device_rows, placed].set(target_slot.reshape(device_total, -1), mode='drop')
    counts = jnp.sum(kept_flat.astype(jnp.int32), axis=1)
    index_x = jnp.arange(GX, dtype=jnp.int32)
    band_index = index_x // (LY * LAYERS_Z)
    row_y = index_x // LAYERS_Z % LY
    layer_index = index_x % LAYERS_Z
    site_low = (band_index * LY + row_y) * LAYERS_Z + layer_index
    site_high = ((LX - REACH + band_index) * LY + row_y) * LAYERS_Z + layer_index
    list_x = jnp.concatenate([slot_of[:, site_low], slot_of[:, site_high]], axis=1)
    index_y = jnp.arange(GY, dtype=jnp.int32)
    column = index_y // (REACH * LAYERS_Z) - REACH
    band_y = index_y // LAYERS_Z % REACH
    layer_y = index_y % LAYERS_Z
    list_y = jnp.concatenate([section_index(slot_of, column, band_y, layer_y), section_index(slot_of, column, LY - REACH + band_y, layer_y)], axis=1)
    return (first_end, second_end, counts, list_x, list_y, site_order)


def draw_positions(key, part):
    tables = lattice_tables(key)
    site_order = tables[5]
    device_total = N_GX * N_GY
    device_ids = jnp.arange(device_total, dtype=jnp.int32)
    column_x = (device_ids // N_GY)[:, None]
    column_y = (device_ids % N_GY)[:, None]
    cell_x = site_order // (LY * LAYERS_Z)
    cell_y = site_order // LAYERS_Z % LY
    cell_z = site_order % LAYERS_Z
    lattice_points = jnp.stack([column_x * LX + cell_x, column_y * LY + cell_y, cell_z]).astype(jnp.float32) * lattice_step
    noise_key = jax.random.fold_in(key, 104)
    jitter = jnp.clip(0.1 * jax.random.normal(noise_key, lattice_points.shape, jnp.float32), -0.25, 0.25)
    return (lattice_points + jitter).reshape(3, -1)


def draw_edge_list(key, part):
    tables = lattice_tables(key)
    return jnp.stack([tables[0], tables[1]]).reshape(2, -1)


def draw_edge_count(key, part):
    return lattice_tables(key)[2]


def draw_send_list_x(key, part):
    return lattice_tables(key)[3].reshape(-1)


def draw_send_list_y(key, part):
    return lattice_tables(key)[4].reshape(-1)


def place_ends(values, rng, least, top_value):
    longest = values.shape.index(max(values.shape))
    spots = []
    for shift in (0, 1):
        where = [jax.random.randint(jax.random.fold_in(rng, axis), (), 0, length) for axis, length in enumerate(values.shape)]
        where[longest] = (where[longest] + shift) % values.shape[longest]
        spots.append(tuple(where))
    return values.at[spots[0]].set(least).at[spots[1]].set(top_value)


def levels(stream_key, dims, cuts, least, high):
    def one(dim, blocks):
        heights = jax.random.uniform(jax.random.fold_in(jax.random.fold_in(stream_key, 6), dim), (blocks,), jnp.float32, least / len(cuts), high / len(cuts))
        return jnp.repeat(jnp.exp(heights), dims[dim] // blocks).reshape((-1,) + (1,) * (len(dims) - dim - 1))

    level = one(*cuts[0])
    for cut in cuts[1:]:
        level = level * one(*cut)
    return level


def bell_draw(key, dims, spread, bound, cuts=(), held_as=jnp.bfloat16):
    values = jax.random.normal(key, dims, jnp.float32) * spread
    if len(cuts) > 0:
        values = levels(key, dims, cuts, -0.22, 0.18) * values
    return jnp.clip(values, min=-bound, max=bound).astype(held_as)


def setup_inputs(seed: int = 0) -> dict:
    streams_of = jax.random.split(jax.random.key(seed), 13)
    positions = draw_positions(jax.random.fold_in(streams_of[12], 71), 0)
    features = bell_draw(streams_of[1], (CHANNELS, ATOMS), 1.0, 6.0, ((1, 256),))
    species = place_ends(jax.random.randint(streams_of[2], (ATOMS,), 0, SPECIES), jax.random.fold_in(streams_of[2], 1), 0, SPECIES - 1).astype(jnp.int32)
    edge_list = draw_edge_list(jax.random.fold_in(streams_of[12], 71), 0)
    edge_count = draw_edge_count(jax.random.fold_in(streams_of[12], 71), 0)
    send_list_x = draw_send_list_x(jax.random.fold_in(streams_of[12], 71), 0)
    send_list_y = draw_send_list_y(jax.random.fold_in(streams_of[12], 71), 0)
    radial_in = bell_draw(streams_of[7], (RADIAL_HIDDEN, RADIAL_BASIS), 2.0, 12.0, (), jnp.float32)
    radial_out = bell_draw(streams_of[8], (3 * CHANNELS, RADIAL_HIDDEN), RADIAL_HIDDEN ** -0.5, 0.75, (), jnp.float32)
    mix_weight = bell_draw(streams_of[9], (CHANNELS, 3 * CHANNELS), (3 * CHANNELS) ** -0.5, 0.4375, (), jnp.float32)
    out_weight = bell_draw(streams_of[10], (CHANNELS,), CHANNELS ** -0.5, 0.75, (), jnp.float32)
    species_energy = bell_draw(streams_of[11], (SPECIES,), 1.0, 6.0, (), jnp.float32)
    return dict(positions=positions, features=features, species=species, edge_list=edge_list, edge_count=edge_count, send_list_x=send_list_x, send_list_y=send_list_y, radial_in=radial_in, radial_out=radial_out, mix_weight=mix_weight, out_weight=out_weight, species_energy=species_energy)


cutoff_radius = 5.0
message_scale = 0.3
degree_of = np.array([0, 1, 1, 1, 2, 2, 2, 2, 2], np.int32)
parity_sign = np.array([1.0, -1.0, -1.0, -1.0, 1.0, 1.0, 1.0, 1.0, 1.0], np.float32)
highest = lax.Precision.HIGHEST

def harmonics(direction):
    along_x, along_y, along_z = (direction[0], direction[1], direction[2])
    root_three = math.sqrt(3.0)
    root_five = math.sqrt(5.0)
    root_fifteen = math.sqrt(15.0)
    return jnp.stack([jnp.ones_like(along_x), root_three * along_x, root_three * along_y, root_three * along_z, root_fifteen * along_x * along_y, root_fifteen * along_y * along_z, 0.5 * root_five * (3.0 * along_z * along_z - 1.0), root_fifteen * along_x * along_z, 0.5 * root_fifteen * (along_x * along_x - along_y * along_y)])

def edge_messages(relative, live_mask, own_features, other_features, radial_in, radial_out):
    distance = jnp.sqrt(lax.optimization_barrier(jnp.sum(relative * relative, axis=0)))
    direction = relative / distance
    orders = jnp.arange(1, radial_in.shape[1] + 1, dtype=jnp.float32)[:, None]
    bessel = math.sqrt(2.0 / cutoff_radius) * jnp.sin(orders * (math.pi / cutoff_radius) * distance) / distance
    scaled = distance / cutoff_radius
    envelope = jnp.where(distance < cutoff_radius, (1.0 - scaled * scaled) ** 2, 0.0)
    hidden = jax.nn.silu(jnp.dot(radial_in, bessel, precision=highest))
    radial = jnp.dot(radial_out, hidden, precision=highest) * (envelope * live_mask)
    channels = own_features.shape[0]
    edge_total = distance.shape[0]
    radial = radial.reshape(3, channels, edge_total)[degree_of]
    shapes = harmonics(direction) * message_scale
    toward_own = shapes[:, None, :] * radial * other_features[None]
    toward_other = (shapes * parity_sign[:, None])[:, None, :] * radial * own_features[None]
    return (toward_own.reshape(9 * channels, edge_total), toward_other.reshape(9 * channels, edge_total))

def atom_energy(partial_value, feature_rows, mix_weight, out_weight):
    channels = feature_rows.shape[0]
    cube = partial_value.reshape(9, channels, -1)
    square = cube * cube
    invariant = jnp.concatenate([square[0], lax.optimization_barrier(jnp.sum(square[1:4], axis=0)), lax.optimization_barrier(jnp.sum(square[4:9], axis=0))], axis=0)
    mixed = jnp.dot(mix_weight, invariant, precision=highest) + feature_rows
    return jnp.dot(out_weight, jax.nn.silu(mixed), precision=highest)

def species_shift(species, species_energy):
    kinds = jnp.arange(species_energy.shape[0], dtype=jnp.int32)
    onehot = (species[None, :] == kinds[:, None]).astype(jnp.float32)
    return jnp.dot(species_energy, onehot, precision=highest)

def ghost_ids(send_list_x, send_list_y):
    device_total = N_GX * N_GY
    own_ids = jnp.arange(device_total * ATOMS_DEV, dtype=jnp.int32).reshape(N_GX, N_GY, ATOMS_DEV)
    picked = jnp.take_along_axis(own_ids, send_list_x.reshape(N_GX, N_GY, 2 * GX), axis=2)
    blank_x = jnp.full((1, N_GY, GX), -1, jnp.int32)
    lower_x = jnp.concatenate([blank_x, picked[:-1, :, GX:]], axis=0)
    upper_x = jnp.concatenate([picked[1:, :, :GX], blank_x], axis=0)
    section_one = jnp.concatenate([own_ids, lower_x, upper_x], axis=2)
    picked_y = jnp.take_along_axis(section_one, send_list_y.reshape(N_GX, N_GY, 2 * GY), axis=2)
    blank_y = jnp.full((N_GX, 1, GY), -1, jnp.int32)
    lower_y = jnp.concatenate([blank_y, picked_y[:, :-1, GY:]], axis=1)
    upper_y = jnp.concatenate([picked_y[:, 1:, :GY], blank_y], axis=1)
    return jnp.concatenate([section_one, lower_y, upper_y], axis=2).reshape(device_total, -1)

def reference(positions, features, species, edge_list, edge_count, send_list_x, send_list_y, radial_in, radial_out, mix_weight, out_weight, species_energy):
    device_total = N_GX * N_GY
    slot_ids = ghost_ids(send_list_x, send_list_y)
    pair_rows = edge_list.reshape(2, device_total, EDGES_DEV)
    first_end = jnp.take_along_axis(slot_ids, pair_rows[0], axis=1)
    second_end = jnp.take_along_axis(slot_ids, pair_rows[1], axis=1)
    live = jnp.arange(EDGES_DEV, dtype=jnp.int32)[None, :] < edge_count[:, None]
    first_end = jnp.where(live, first_end, 0).astype(jnp.int32)
    second_end = jnp.where(live, second_end, 0).astype(jnp.int32)
    feature_rows = features.astype(jnp.float32)
    filler = jnp.array([[2.0], [0.0], [0.0]], jnp.float32)

    def energy_total(coords):

        def advance(partial_value, block_data):
            first_row, second_row, live_row = block_data
            relative = coords[:, second_row] - coords[:, first_row]
            relative = jnp.where(live_row[None, :], relative, filler)
            toward_first, toward_second = edge_messages(relative, live_row.astype(jnp.float32), feature_rows[:, first_row], feature_rows[:, second_row], radial_in, radial_out)
            partial_value = partial_value.at[:, first_row].add(toward_first).at[:, second_row].add(toward_second)
            return (partial_value, None)
        start_sums = jnp.zeros((9 * feature_rows.shape[0], feature_rows.shape[1]), jnp.float32)
        partial_value, ignored = lax.scan(jax.checkpoint(advance), start_sums, (first_end, second_end, live))
        energy = atom_energy(partial_value, feature_rows, mix_weight, out_weight)
        return (jnp.sum(energy), energy)
    (ignored, energy), gradient = jax.value_and_grad(energy_total, has_aux=True)(positions)
    return (energy + species_shift(species, species_energy), -gradient)
```

```python
import functools
import math

import jax
import jax.numpy as jnp
from jax import lax
from jax.experimental import pallas as pl
from jax.experimental.pallas import tpu as pltpu
from jax.sharding import PartitionSpec as P

MESH = pl.DeviceIdType.MESH
F32 = jnp.float32
BF16 = jnp.bfloat16
HIGHEST = lax.Precision.HIGHEST

CH = 64
OWN = 128
GX = 64
GY = 32
EXT = 320
EXT_PAD = 384
TILE = 256
STEPS = 13
SLOTS = TILE * STEPS
ROWS = 9 * CH
ROWS_PAD = 640

CUTOFF = 5.0
SCALE = 0.3
S3 = math.sqrt(3.0)
S5 = math.sqrt(5.0)
S15 = math.sqrt(15.0)
DEGREE = (0, 1, 1, 1, 2, 2, 2, 2, 2)
PARITY = (1.0, -1.0, -1.0, -1.0, 1.0, 1.0, 1.0, 1.0, 1.0)

NN = (((1,), (0,)), ((), ()))
NT = (((1,), (1,)), ((), ()))


def mm(a, b, dims=NN, precision=None):
    return lax.dot_general(a, b, dims, precision=precision, preferred_element_type=F32)


def split2(x):
    hi = x.astype(BF16)
    return hi, (x - hi.astype(F32)).astype(BF16)


def split3(x):
    a = x.astype(BF16).astype(F32)
    b = (x - a).astype(BF16).astype(F32)
    return a, b, (x - a) - b


def iota(shape, dim):
    return lax.broadcasted_iota(jnp.int32, shape, dim)


def onehot(cond):
    return jnp.where(cond, 1.0, 0.0)


def sin_cos(arg):
    k = jnp.floor(arg * (1.0 / math.pi) + 0.5)
    r = (arg - k * 3.140625) - k * (math.pi - 3.140625)
    sign = 1.0 - 2.0 * (k - 2.0 * jnp.floor(k * 0.5))
    r2 = r * r
    s = 1.0 / 6227020800.0
    for c in (-1.0 / 39916800, 1.0 / 362880, -1.0 / 5040, 1.0 / 120, -1.0 / 6, 1.0):
        s = s * r2 + c
    q = -1.0 / 87178291200.0
    for c in (1.0 / 479001600, -1.0 / 3628800, 1.0 / 40320, -1.0 / 720, 1.0 / 24, -0.5, 1.0):
        q = q * r2 + c
    return sign * (s * r), sign * q


def body(
    comm,
    n_gx,
    n_gy,
    pos_ref,
    feat_ref,
    spec_ref,
    edge_ref,
    cnt_ref,
    slx_ref,
    sly_ref,
    win_ref,
    wout_ref,
    mix_ref,
    outw_ref,
    se_ref,
    energy_ref,
    force_ref,
    pos8,
    slyp,
    oh1,
    oh2,
    send_a,
    recv_a,
    ext_l,
    pa_s,
    fa_s,
    fb_s,
    geo,
    r_s,
    rp_s,
    w3,
    m_s,
    s1,
    s2,
    rsy,
    rsx,
    gown,
    gext,
    sgx,
    rgx,
    sgy,
    rgy,
    zacc,
    facc,
    send_f,
    recv_f,
    send_sem,
    recv_sem,
):
    if comm:
        ix = lax.axis_index("gx")
        iy = lax.axis_index("gy")
        x_low = (lax.rem(ix + n_gx - 1, n_gx), iy)
        x_high = (lax.rem(ix + 1, n_gx), iy)
        y_low = (ix, lax.rem(iy + n_gy - 1, n_gy))
        y_high = (ix, lax.rem(iy + 1, n_gy))
        barrier = pltpu.get_barrier_semaphore()
        for device in (x_low, x_high, y_low, y_high):
            pl.semaphore_signal(barrier, inc=1, device_id=device, device_id_type=MESH)
    else:
        x_low = x_high = y_low = y_high = None

    def push(number, src, dst, device):
        if not comm:
            return None
        copy = pltpu.make_async_remote_copy(
            src_ref=src,
            dst_ref=dst,
            send_sem=send_sem.at[number],
            recv_sem=recv_sem.at[number],
            device_id=device,
            device_id_type=MESH,
        )
        copy.start()
        return copy

    def settle(*copies):
        for copy in copies:
            if copy is not None:
                copy.wait()

    lane = iota((1, OWN), 1)

    slyp[...] = jnp.full_like(slyp, -1)
    slyp[:, 0 : 2 * GY] = sly_ref[...]
    ohx_t32 = onehot(iota((OWN, OWN), 0) == slx_ref[...])
    ohy_t32 = onehot(iota((2 * OWN, OWN), 0) == slyp[...])
    ohx_t = ohx_t32.astype(BF16)
    ohy_t = ohy_t32.astype(BF16)
    ohx = ohx_t32.T.astype(BF16)
    ohy = ohy_t32.T.astype(BF16)

    def pack(rows72):
        a, b, c = split3(rows72[CH : CH + 8])
        pieces = jnp.concatenate([a, b, c, jnp.zeros_like(a)], axis=0).astype(BF16)
        return jnp.concatenate([rows72[:CH].astype(BF16), pieces], axis=0)

    def unpack(rows96):
        return (rows96[CH : CH + 8] + rows96[CH + 8 : CH + 16]) + rows96[CH + 16 : CH + 24]

    def fold_x(low, high):
        return jnp.where(lane < GX, pltpu.roll(low, GX, 1), pltpu.roll(high, GX, 1))

    def fold_y(low, high):
        picked = jnp.where(lane < GY, pltpu.roll(low, OWN - GY, 1), pltpu.roll(high, GY, 1))
        return jnp.where(lane < 2 * GY, picked, 0.0)

    pos8[...] = jnp.zeros_like(pos8)
    pos8[0:3, :] = pos_ref[...]
    own_l = pack(jnp.concatenate([feat_ref[...].astype(F32), pos8[...]], axis=0))
    ext_l[:, 0:OWN] = own_l
    picked = mm(own_l, ohx_t)
    send_a[0, 0:CH, :] = picked[0:CH]
    send_a[0, CH : CH + 8, :] = unpack(picked)
    if comm:
        pl.semaphore_wait(barrier, 4)
    c0 = push(0, send_a.at[0], recv_a.at[1], x_low)
    c1 = push(1, send_a.at[0], recv_a.at[0], x_high)

    w_hi, w_lo = split2(wout_ref[...])
    col = iota((CH, 3 * CH), 1)
    row = iota((CH, 3 * CH), 0)
    place_hi = onehot((col == row) | (col == row + CH)).astype(BF16)
    place_lo = onehot(col == row + 2 * CH).astype(BF16)
    w3[...] = (mm(w_hi, place_hi) + mm(w_lo, place_lo)).astype(BF16)
    count = cnt_ref[0]

    def table_step(step, carry):
        at = pl.ds(pl.multiple_of(step * TILE, TILE), TILE)
        live = iota((1, TILE), 1) + step * TILE < count
        first = jnp.where(live, edge_ref[0:1, at], -1)
        second = jnp.where(live, edge_ref[1:2, at], -1)
        table1 = onehot(iota((OWN, TILE), 0) == first).astype(BF16)
        oh1[:, at] = table1
        oh2[:, at] = onehot(iota((EXT_PAD, TILE), 0) == second).astype(BF16)
        got = mm(ext_l[:, 0:OWN], table1)
        fa_s[:, at] = got[0:CH]
        pa_s[:, at] = unpack(got)
        return carry

    lax.fori_loop(0, STEPS, table_step, 0)

    settle(c0, c1)
    if comm:
        section = pack(fold_x(recv_a[0], recv_a[1]))
    else:
        section = own_l
    ext_l[:, OWN : 2 * OWN] = section
    picked = mm(own_l, ohy_t[0:OWN]) + mm(section, ohy_t[OWN : 2 * OWN])
    send_a[1, 0:CH, :] = picked[0:CH]
    send_a[1, CH : CH + 8, :] = unpack(picked)
    c0 = push(2, send_a.at[1], recv_a.at[3], y_low)
    c1 = push(3, send_a.at[1], recv_a.at[2], y_high)
    settle(c0, c1)
    if comm:
        ext_l[:, 2 * OWN : 3 * OWN] = pack(fold_y(recv_a[2], recv_a[3]))
    else:
        ext_l[:, 2 * OWN : 3 * OWN] = jnp.where(lane < 2 * GY, own_l, 0.0)

    s1[...] = jnp.zeros_like(s1)
    s2[...] = jnp.zeros_like(s2)
    m_s[ROWS:ROWS_PAD, :] = jnp.zeros((ROWS_PAD - ROWS, TILE), BF16)
    m_s[ROWS_PAD + ROWS :, :] = jnp.zeros((ROWS_PAD - ROWS, TILE), BF16)

    def messages(shapes, radial, features):
        for degree in range(3):
            product = radial[degree * CH : (degree + 1) * CH] * features
            for q in range(9):
                if DEGREE[q] != degree:
                    continue
                hi, lo = split2(shapes[q] * product)
                m_s[q * CH : (q + 1) * CH, :] = hi
                m_s[ROWS_PAD + q * CH : ROWS_PAD + (q + 1) * CH, :] = lo

    def first_step(step, carry):
        at = pl.ds(pl.multiple_of(step * TILE, TILE), TILE)
        live = iota((1, TILE), 1) + step * TILE < count
        got = mm(ext_l[...], oh2[:, at])
        fb_s[:, at] = got[0:CH]
        relative = unpack(got) - pa_s[:, at]
        rx = jnp.where(live, relative[0:1], 2.0)
        ry = jnp.where(live, relative[1:2], 0.0)
        rz = jnp.where(live, relative[2:3], 0.0)
        d = jnp.sqrt(rx * rx + ry * ry + rz * rz)
        inv = 1.0 / d
        x, y, z = rx * inv, ry * inv, rz * inv
        scaled = d * (1.0 / CUTOFF)
        left = 1.0 - scaled * scaled
        inside = d < CUTOFF
        env = jnp.where(inside, left * left, 0.0)
        env_d = jnp.where(inside, (-4.0 / CUTOFF) * scaled * left, 0.0)
        shapes = [
            jnp.full_like(x, SCALE),
            (SCALE * S3) * x,
            (SCALE * S3) * y,
            (SCALE * S3) * z,
            (SCALE * S15) * (x * y),
            (SCALE * S15) * (y * z),
            (SCALE * 0.5 * S5) * (3.0 * z * z - 1.0),
            (SCALE * S15) * (x * z),
            (SCALE * 0.5 * S15) * (x * x - y * y),
        ]
        for number, value in enumerate(shapes + [x, y, z, inv]):
            geo[number : number + 1, at] = value
        order = (iota((8, TILE), 0) + 1).astype(F32)
        sine, cosine = sin_cos(order * (d * (math.pi / CUTOFF)))
        root = math.sqrt(2.0 / CUTOFF)
        bessel = root * sine * inv
        bessel_d = (root * (math.pi / CUTOFF) * order * cosine - bessel) * inv
        both = mm(win_ref[...], jnp.concatenate([bessel, bessel_d], axis=1), precision=HIGHEST)
        u, u_d = both[:, :TILE], both[:, TILE:]
        gate = 1.0 / (1.0 + jnp.exp(-u))
        hidden = u * gate
        slope = gate * (1.0 + u * (1.0 - gate))
        g = jnp.concatenate([env * hidden, env_d * hidden + env * (slope * u_d)], axis=1)
        hi, lo = split2(g)
        radial = mm(w3[...], jnp.concatenate([hi, lo, hi], axis=0))
        r_s[:, at] = radial[:, :TILE]
        rp_s[:, at] = radial[:, TILE:]
        messages(
            [PARITY[q] * shapes[q] for q in range(9)], radial[:, :TILE], fa_s[:, at]
        )
        out = mm(oh2[0:EXT, at], m_s[...], NT)
        s2[...] += out[:, :ROWS] + out[:, ROWS_PAD : ROWS_PAD + ROWS]
        return carry

    lax.fori_loop(0, STEPS, first_step, 0)

    c0 = push(4, s2.at[pl.ds(2 * OWN, GY)], rsy.at[pl.ds(GY, GY)], y_low)
    c1 = push(5, s2.at[pl.ds(2 * OWN + GY, GY)], rsy.at[pl.ds(0, GY)], y_high)

    def second_step(step, carry):
        at = pl.ds(pl.multiple_of(step * TILE, TILE), TILE)
        messages([geo[q : q + 1, at] for q in range(9)], r_s[:, at], fb_s[:, at])
        out = mm(oh1[:, at], m_s[...], NT)
        s1[...] += out[:, :ROWS] + out[:, ROWS_PAD : ROWS_PAD + ROWS]
        return carry

    lax.fori_loop(0, STEPS // 2, second_step, 0)
    settle(c0, c1)
    if comm:
        hi, lo = split2(rsy[...])
        s2[0 : 2 * OWN, :] += mm(ohy_t[:, 0 : 2 * GY], hi) + mm(ohy_t[:, 0 : 2 * GY], lo)
    c0 = push(6, s2.at[pl.ds(OWN, GX)], rsx.at[pl.ds(GX, GX)], x_low)
    c1 = push(7, s2.at[pl.ds(OWN + GX, GX)], rsx.at[pl.ds(0, GX)], x_high)
    lax.fori_loop(STEPS // 2, STEPS, second_step, 0)
    settle(c0, c1)
    sums_t = s2[0:OWN, :] + s1[...]
    if comm:
        hi, lo = split2(rsx[...])
        sums_t = sums_t + mm(ohx_t, hi) + mm(ohx_t, lo)

    sums = sums_t.T
    squares = [sums[q * CH : (q + 1) * CH] * sums[q * CH : (q + 1) * CH] for q in range(9)]
    invariant = jnp.concatenate(
        [
            squares[0],
            squares[1] + squares[2] + squares[3],
            squares[4] + squares[5] + squares[6] + squares[7] + squares[8],
        ],
        axis=0,
    )
    mixed = mm(mix_ref[...], invariant, precision=HIGHEST) + feat_ref[...].astype(F32)
    gate = 1.0 / (1.0 + jnp.exp(-mixed))
    diagonal = iota((CH, CH), 0) == iota((CH, CH), 1)
    weight = jnp.sum(jnp.where(diagonal, outw_ref[...], 0.0), axis=1, keepdims=True)
    energy = jnp.sum(weight * (mixed * gate), axis=0, keepdims=True)
    kind = spec_ref[...]
    shift = jnp.zeros_like(energy)
    for k in range(5):
        shift = jnp.where(kind == k, se_ref[k], shift)
    energy_ref[...] = energy + shift
    d_mixed = weight * (gate * (1.0 + mixed * (1.0 - gate)))
    d_inv = 2.0 * mm(mix_ref[...].T, d_mixed, precision=HIGHEST)
    gext[...] = jnp.zeros_like(gext)
    for q in range(9):
        at = slice(q * CH, (q + 1) * CH)
        gradient = sums[at] * d_inv[DEGREE[q] * CH : (DEGREE[q] + 1) * CH]
        hi, lo = split2(gradient)
        gown[at, 0:OWN] = hi
        gown[at, OWN : 2 * OWN] = lo
        hi, lo = split2(PARITY[q] * gradient)
        gext[at, 0:OWN] = hi
        gext[at, EXT_PAD : EXT_PAD + OWN] = lo

    def own_rows(table):
        return mm(table, gext[:, 0:OWN], NT) + mm(table, gext[:, EXT_PAD : EXT_PAD + OWN], NT)

    sgx[...] = own_rows(ohx)
    c0 = push(8, sgx.at[pl.ds(0, GX)], rgx.at[pl.ds(GX, GX)], x_low)
    c1 = push(9, sgx.at[pl.ds(GX, GX)], rgx.at[pl.ds(0, GX)], x_high)
    outgoing_y = own_rows(ohy[0 : 2 * GY, 0:OWN])

    def store_ghosts(rows, start):
        hi, lo = split2(rows.T)
        count_here = rows.shape[0]
        gext[:, start : start + count_here] = hi
        gext[:, EXT_PAD + start : EXT_PAD + start + count_here] = lo

    def contract(step, gathered, features):
        at = pl.ds(pl.multiple_of(step * TILE, TILE), TILE)
        along = jnp.zeros((CH, TILE), F32)
        rows_z = []
        for degree in range(3):
            radial = r_s[degree * CH : (degree + 1) * CH, at]
            total = None
            for q in range(9):
                if DEGREE[q] != degree:
                    continue
                product = gathered[q * CH : (q + 1) * CH] * features
                rows_z.append(jnp.sum(radial * product, axis=0, keepdims=True))
                term = geo[q : q + 1, at] * product
                total = term if total is None else total + term
            along = along + rp_s[degree * CH : (degree + 1) * CH, at] * total
        rows_z.append(jnp.sum(along, axis=0, keepdims=True))
        return rows_z

    def own_step(step, carry):
        at = pl.ds(pl.multiple_of(step * TILE, TILE), TILE)
        table = oh1[:, at]
        gathered = mm(gown[...], jnp.concatenate([table, table], axis=0))
        rows_z = contract(step, gathered, fb_s[:, at])
        for number, value in enumerate(rows_z):
            zacc[number : number + 1, at] = value
        return carry

    lax.fori_loop(0, 8, own_step, 0)
    settle(c0, c1)
    if comm:
        hi, lo = split2(rgx[...])
        table = ohy[0 : 2 * GY, OWN : 2 * OWN]
        sgy[...] = outgoing_y + mm(table, hi) + mm(table, lo)
    c0 = push(10, sgy.at[pl.ds(0, GY)], rgy.at[pl.ds(GY, GY)], y_low)
    c1 = push(11, sgy.at[pl.ds(GY, GY)], rgy.at[pl.ds(0, GY)], y_high)
    if comm:
        store_ghosts(rgx[...], OWN)
    lax.fori_loop(8, STEPS, own_step, 0)
    settle(c0, c1)
    if comm:
        store_ghosts(rgy[...], 2 * OWN)

    facc[...] = jnp.zeros_like(facc)

    def last_step(step, carry):
        at = pl.ds(pl.multiple_of(step * TILE, TILE), TILE)
        table = oh2[:, at]
        gathered = mm(gext[...], jnp.concatenate([table, table], axis=0))
        rows_z = contract(step, gathered, fa_s[:, at])
        z = [rows_z[q] + zacc[q : q + 1, at] for q in range(10)]
        nx, ny, nz = geo[9:10, at], geo[10:11, at], geo[11:12, at]
        inv = geo[12:13, at]
        gx = S3 * z[1] + S15 * (ny * z[4] + nz * z[7] + nx * z[8])
        gy = S3 * z[2] + S15 * (nx * z[4] + nz * z[5] - ny * z[8])
        gz = S3 * z[3] + S15 * (ny * z[5] + nx * z[7]) + (3.0 * S5) * (nz * z[6])
        factor = SCALE * inv
        gx, gy, gz = gx * factor, gy * factor, gz * factor
        radial_part = z[9] - (gx * nx + gy * ny + gz * nz)
        zero = jnp.zeros((5, TILE), F32)
        pulled = jnp.concatenate(
            [gx + radial_part * nx, gy + radial_part * ny, gz + radial_part * nz, zero], axis=0
        )
        hi = pulled.astype(BF16).astype(F32)
        pieces = jnp.concatenate([hi, pulled - hi], axis=0).astype(BF16)
        facc[...] -= mm(table, pieces, NT)
        facc[0:OWN, :] += mm(oh1[:, at], pieces, NT)
        return carry

    lax.fori_loop(0, STEPS, last_step, 0)

    def home(rows8, table):
        a, b, c = split3(rows8)
        out = mm(jnp.concatenate([a, b, c, jnp.zeros_like(a)], axis=0).astype(BF16), table)
        return out[0:8] + out[8:16] + out[16:24]

    total = facc[...].T
    total = total[0:8] + total[8:16]
    send_f[0] = total[:, 2 * OWN : 3 * OWN]
    c0 = push(12, send_f.at[0], recv_f.at[1], y_low)
    c1 = push(13, send_f.at[0], recv_f.at[0], y_high)
    settle(c0, c1)
    near = total[:, 0 : 2 * OWN]
    if comm:
        near = near + home(fold_y(recv_f[0], recv_f[1]), ohy)
    send_f[1] = near[:, OWN : 2 * OWN]
    c0 = push(14, send_f.at[1], recv_f.at[3], x_low)
    c1 = push(15, send_f.at[1], recv_f.at[2], x_high)
    settle(c0, c1)
    own = near[:, 0:OWN]
    if comm:
        own = own + home(fold_x(recv_f[2], recv_f[3]), ohx)
    force_ref[...] = own[0:3]


def run(args, n_gx, n_gy, comm=True):
    (
        positions,
        features,
        species,
        edge_list,
        edge_count,
        send_list_x,
        send_list_y,
        radial_in,
        radial_out,
        mix_weight,
        out_weight,
        species_energy,
    ) = args
    vmem = pl.BlockSpec(memory_space=pltpu.VMEM)
    smem = pl.BlockSpec(memory_space=pltpu.SMEM)
    scratch = [
        pltpu.VMEM((8, OWN), F32),
        pltpu.VMEM((1, OWN), jnp.int32),
        pltpu.VMEM((OWN, SLOTS), BF16),
        pltpu.VMEM((EXT_PAD, SLOTS), BF16),
        pltpu.VMEM((2, CH + 8, OWN), F32),
        pltpu.VMEM((4, CH + 8, OWN), F32),
        pltpu.VMEM((CH + 32, EXT_PAD), BF16),
        pltpu.VMEM((8, SLOTS), F32),
        pltpu.VMEM((CH, SLOTS), F32),
        pltpu.VMEM((CH, SLOTS), F32),
        pltpu.VMEM((16, SLOTS), F32),
        pltpu.VMEM((3 * CH, SLOTS), F32),
        pltpu.VMEM((3 * CH, SLOTS), F32),
        pltpu.VMEM((3 * CH, 3 * CH), BF16),
        pltpu.VMEM((2 * ROWS_PAD, TILE), BF16),
        pltpu.VMEM((OWN, ROWS), F32),
        pltpu.VMEM((EXT, ROWS), F32),
        pltpu.VMEM((2 * GY, ROWS), F32),
        pltpu.VMEM((2 * GX, ROWS), F32),
        pltpu.VMEM((ROWS, 2 * OWN), BF16),
        pltpu.VMEM((ROWS, 2 * EXT_PAD), BF16),
        pltpu.VMEM((2 * GX, ROWS), F32),
        pltpu.VMEM((2 * GX, ROWS), F32),
        pltpu.VMEM((2 * GY, ROWS), F32),
        pltpu.VMEM((2 * GY, ROWS), F32),
        pltpu.VMEM((16, SLOTS), F32),
        pltpu.VMEM((EXT_PAD, 16), F32),
        pltpu.VMEM((2, 8, OWN), F32),
        pltpu.VMEM((4, 8, OWN), F32),
        pltpu.SemaphoreType.DMA((16,)),
        pltpu.SemaphoreType.DMA((16,)),
    ]
    params = {"collective_id": 0, "has_side_effects": True} if comm else {}
    energies, forces = pl.pallas_call(
        functools.partial(body, comm, n_gx, n_gy),
        out_shape=(
            jax.ShapeDtypeStruct((1, OWN), F32),
            jax.ShapeDtypeStruct((3, OWN), F32),
        ),
        in_specs=[vmem, vmem, vmem, vmem, smem, vmem, vmem, vmem, vmem, vmem, vmem, smem],
        out_specs=(vmem, vmem),
        scratch_shapes=scratch,
        compiler_params=pltpu.CompilerParams(vmem_limit_bytes=60 * 1024 * 1024, **params),
        name="layer",
    )(
        positions,
        features,
        species.reshape(1, -1),
        edge_list,
        edge_count,
        send_list_x.reshape(1, -1),
        send_list_y.reshape(1, -1),
        radial_in,
        radial_out,
        mix_weight,
        out_weight.reshape(1, -1),
        species_energy,
    )
    return energies.reshape(-1), forces


def solution(mesh):
    n_gx, n_gy = mesh.shape["gx"], mesh.shape["gy"]
    both = ("gx", "gy")
    placed = (
        P(None, both),
        P(None, both),
        P(both),
        P(None, both),
        P(both),
        P(both),
        P(both),
        P(),
        P(),
        P(),
        P(),
        P(),
    )
    return jax.shard_map(
        lambda *args: run(args, n_gx, n_gy),
        mesh=mesh,
        in_specs=placed,
        out_specs=(P(both), P(None, both)),
        check_vma=False,
    )
```

```python
import functools
import math

import jax
import jax.numpy as jnp
from jax import lax
from jax.experimental import pallas as pl
from jax.experimental.pallas import tpu as pltpu
from jax.sharding import PartitionSpec as P

MESH = pl.DeviceIdType.MESH
F32 = jnp.float32
BF16 = jnp.bfloat16
HIGHEST = lax.Precision.HIGHEST

CH = 64
OWN = 128
GX = 64
GY = 32
EXT = 320
EXT_PAD = 384
TILE = 256
STEPS = 13
SLOTS = TILE * STEPS
ROWS = 9 * CH
DENSE = 32

CUTOFF = 5.0
SCALE = 0.3
S3 = math.sqrt(3.0)
S5 = math.sqrt(5.0)
S15 = math.sqrt(15.0)
DEGREE = (0, 1, 1, 1, 2, 2, 2, 2, 2)
PARITY = (1.0, -1.0, -1.0, -1.0, 1.0, 1.0, 1.0, 1.0, 1.0)

UNROLL_GATHER = 1
UNROLL_RADIAL = 1
UNROLL_SUMS = 1
UNROLL_BACK = 1

NN = (((1,), (0,)), ((), ()))
NT = (((1,), (1,)), ((), ()))


def mm(a, b, dims=NN, precision=None):
    return lax.dot_general(a, b, dims, precision=precision, preferred_element_type=F32)


def split2(x):
    hi = x.astype(BF16)
    return hi, (x - hi.astype(F32)).astype(BF16)


def split3(x):
    a = x.astype(BF16).astype(F32)
    b = (x - a).astype(BF16).astype(F32)
    return a, b, (x - a) - b


def iota(shape, dim):
    return lax.broadcasted_iota(jnp.int32, shape, dim)


def onehot(cond):
    return jnp.where(cond, 1.0, 0.0)


def sin_cos(arg):
    k = jnp.floor(arg * (1.0 / math.pi) + 0.5)
    r = (arg - k * 3.140625) - k * (math.pi - 3.140625)
    sign = 1.0 - 2.0 * (k - 2.0 * jnp.floor(k * 0.5))
    r2 = r * r
    s = 1.0 / 6227020800.0
    for c in (-1.0 / 39916800, 1.0 / 362880, -1.0 / 5040, 1.0 / 120, -1.0 / 6, 1.0):
        s = s * r2 + c
    q = -1.0 / 87178291200.0
    for c in (1.0 / 479001600, -1.0 / 3628800, 1.0 / 40320, -1.0 / 720, 1.0 / 24, -0.5, 1.0):
        q = q * r2 + c
    return sign * (s * r), sign * q


def body(
    comm,
    n_gx,
    n_gy,
    pos_ref,
    feat_ref,
    spec_ref,
    edge_ref,
    cnt_ref,
    slx_ref,
    sly_ref,
    win_ref,
    wout_ref,
    mix_ref,
    outw_ref,
    se_ref,
    energy_ref,
    force_ref,
    pos8,
    slyp,
    oh1,
    oh2,
    send_a,
    recv_a,
    ext_l,
    pa_s,
    rel_d,
    bes_d,
    slope_d,
    geo_d,
    pull_d,
    fa_s,
    fb_s,
    r_s,
    rp_s,
    w3,
    w6,
    m_s,
    s1,
    s2,
    rsy,
    rsx,
    gown,
    gext,
    sgx,
    rgx,
    sgy,
    rgy,
    z_own,
    z_ext,
    pieces_s,
    send_f,
    recv_f,
    send_sem,
    recv_sem,
):
    if comm:
        ix = lax.axis_index("gx")
        iy = lax.axis_index("gy")
        x_low = (lax.rem(ix + n_gx - 1, n_gx), iy)
        x_high = (lax.rem(ix + 1, n_gx), iy)
        y_low = (ix, lax.rem(iy + n_gy - 1, n_gy))
        y_high = (ix, lax.rem(iy + 1, n_gy))
        barrier = pltpu.get_barrier_semaphore()
        for device in (x_low, x_high, y_low, y_high):
            pl.semaphore_signal(barrier, inc=1, device_id=device, device_id_type=MESH)
    else:
        x_low = x_high = y_low = y_high = None

    def push(number, src, dst, device):
        if not comm:
            return None
        copy = pltpu.make_async_remote_copy(
            src_ref=src,
            dst_ref=dst,
            send_sem=send_sem.at[number],
            recv_sem=recv_sem.at[number],
            device_id=device,
            device_id_type=MESH,
        )
        copy.start()
        return copy

    def settle(*copies):
        for copy in copies:
            if copy is not None:
                copy.wait()

    lane = iota((1, OWN), 1)

    slyp[...] = jnp.full_like(slyp, -1)
    slyp[:, 0 : 2 * GY] = sly_ref[...]
    ohx_t32 = onehot(iota((OWN, OWN), 0) == slx_ref[...])
    ohy_t32 = onehot(iota((2 * OWN, OWN), 0) == slyp[...])
    ohx_t = ohx_t32.astype(BF16)
    ohy_t = ohy_t32.astype(BF16)
    ohx = ohx_t32.T.astype(BF16)
    ohy = ohy_t32.T.astype(BF16)

    def pack(rows72):
        a, b, c = split3(rows72[CH : CH + 8])
        pieces = jnp.concatenate([a, b, c, jnp.zeros_like(a)], axis=0).astype(BF16)
        return jnp.concatenate([rows72[:CH].astype(BF16), pieces], axis=0)

    def unpack(rows96):
        return (rows96[CH : CH + 8] + rows96[CH + 8 : CH + 16]) + rows96[CH + 16 : CH + 24]

    def fold_x(low, high):
        return jnp.where(lane < GX, pltpu.roll(low, GX, 1), pltpu.roll(high, GX, 1))

    def fold_y(low, high):
        picked = jnp.where(lane < GY, pltpu.roll(low, OWN - GY, 1), pltpu.roll(high, GY, 1))
        return jnp.where(lane < 2 * GY, picked, 0.0)

    pos8[...] = jnp.zeros_like(pos8)
    pos8[0:3, :] = pos_ref[...]
    own_l = pack(jnp.concatenate([feat_ref[...].astype(F32), pos8[...]], axis=0))
    ext_l[:, 0:OWN] = own_l
    picked = mm(own_l, ohx_t)
    send_a[0, 0:CH, :] = picked[0:CH]
    send_a[0, CH : CH + 8, :] = unpack(picked)
    if comm:
        pl.semaphore_wait(barrier, 4)
    c0 = push(0, send_a.at[0], recv_a.at[1], x_low)
    c1 = push(1, send_a.at[0], recv_a.at[0], x_high)

    hi, lo = split2(wout_ref[...])
    hi, lo = hi.astype(F32), lo.astype(F32)
    w3[...] = jnp.concatenate([hi, hi, lo], axis=0).T.astype(BF16)
    a, b, c = split3(win_ref[...])
    zero = jnp.zeros_like(a)
    w6[...] = jnp.concatenate([a, a, b, b, a, c, zero, zero], axis=0).T.astype(BF16)
    count = cnt_ref[0]

    def table_step(step, carry):
        at = pl.ds(pl.multiple_of(step * TILE, TILE), TILE)
        live = iota((1, TILE), 1) + step * TILE < count
        first = jnp.where(live, edge_ref[0:1, at], -1)
        second = jnp.where(live, edge_ref[1:2, at], -1)
        table1 = onehot(iota((OWN, TILE), 0) == first).astype(BF16)
        oh1[:, at] = table1
        oh2[:, at] = onehot(iota((EXT_PAD, TILE), 0) == second).astype(BF16)
        got = mm(ext_l[:, 0:OWN], table1)
        fa_s[:, at] = got[0:CH]
        pa_s[:, at] = unpack(got)
        return carry

    lax.fori_loop(0, STEPS, table_step, 0)

    settle(c0, c1)
    if comm:
        section = pack(fold_x(recv_a[0], recv_a[1]))
    else:
        section = own_l
    ext_l[:, OWN : 2 * OWN] = section
    picked = mm(own_l, ohy_t[0:OWN]) + mm(section, ohy_t[OWN : 2 * OWN])
    send_a[1, 0:CH, :] = picked[0:CH]
    send_a[1, CH : CH + 8, :] = unpack(picked)
    c0 = push(2, send_a.at[1], recv_a.at[3], y_low)
    c1 = push(3, send_a.at[1], recv_a.at[2], y_high)
    settle(c0, c1)
    if comm:
        ext_l[:, 2 * OWN : 3 * OWN] = pack(fold_y(recv_a[2], recv_a[3]))
    else:
        ext_l[:, 2 * OWN : 3 * OWN] = jnp.where(lane < 2 * GY, own_l, 0.0)

    def span(step):
        return pl.ds(pl.multiple_of(step * TILE, TILE), TILE)

    def loop(start, stop, step_fn, unroll):
        def one(step, carry):
            step_fn(step)
            return carry

        lax.fori_loop(start, stop, one, 0, unroll=unroll)

    def halves(value):
        return value[:, 0:OWN], value[:, OWN:TILE]

    def get_row(ref, number, step):
        at = number * DENSE + 2 * step
        return jnp.concatenate([ref[pl.ds(at, 1), :], ref[pl.ds(at + 1, 1), :]], axis=1)

    def put_row(ref, number, step, value):
        at = number * DENSE + 2 * step
        low, high = halves(value)
        ref[pl.ds(at, 1), :] = low
        ref[pl.ds(at + 1, 1), :] = high

    def get_eight(ref, step):
        at = 2 * step
        return jnp.concatenate(
            [ref[pl.ds(at, 8, stride=DENSE), :], ref[pl.ds(at + 1, 8, stride=DENSE), :]], axis=1
        )

    def dense(ref, number):
        return ref[number * DENSE : (number + 1) * DENSE, :]

    rel_d[...] = jnp.full_like(rel_d, 2.0)

    def gather_step(step):
        got = mm(ext_l[...], oh2[:, span(step)])
        fb_s[:, span(step)] = got[0:CH]
        relative = unpack(got) - pa_s[:, span(step)]
        for number in range(3):
            put_row(rel_d, number, step, relative[number : number + 1])

    loop(0, STEPS, gather_step, UNROLL_GATHER)

    live = iota((DENSE, OWN), 0) * OWN + iota((DENSE, OWN), 1) < count
    rx = jnp.where(live, dense(rel_d, 0), 2.0)
    ry = jnp.where(live, dense(rel_d, 1), 0.0)
    rz = jnp.where(live, dense(rel_d, 2), 0.0)
    d = jnp.sqrt(rx * rx + ry * ry + rz * rz)
    inv = 1.0 / d
    x, y, z = rx * inv, ry * inv, rz * inv
    scaled = d * (1.0 / CUTOFF)
    left = 1.0 - scaled * scaled
    inside = d < CUTOFF
    values = [
        jnp.full_like(x, SCALE),
        (SCALE * S3) * x,
        (SCALE * S3) * y,
        (SCALE * S3) * z,
        (SCALE * S15) * (x * y),
        (SCALE * S15) * (y * z),
        (SCALE * 0.5 * S5) * (3.0 * z * z - 1.0),
        (SCALE * S15) * (x * z),
        (SCALE * 0.5 * S15) * (x * x - y * y),
        x,
        y,
        z,
        inv,
        jnp.where(inside, left * left, 0.0),
        jnp.where(inside, (-4.0 / CUTOFF) * scaled * left, 0.0),
    ]
    for number, value in enumerate(values):
        geo_d[number * DENSE : (number + 1) * DENSE, :] = value
    sine, cosine = sin_cos(d * (math.pi / CUTOFF))
    twice = 2.0 * cosine
    sine_last, cosine_last = jnp.zeros_like(sine), jnp.ones_like(sine)
    root = math.sqrt(2.0 / CUTOFF)
    for number in range(8):
        bessel = root * sine * inv
        bes_d[number * DENSE : (number + 1) * DENSE, :] = bessel
        slope_d[number * DENSE : (number + 1) * DENSE, :] = (
            (root * (math.pi / CUTOFF) * (number + 1)) * cosine - bessel
        ) * inv
        sine, sine_last = twice * sine - sine_last, sine
        cosine, cosine_last = twice * cosine - cosine_last, cosine

    def radial_step(step):
        basis = jnp.concatenate([get_eight(bes_d, step), get_eight(slope_d, step)], axis=1)
        a, b, c = split3(basis)
        zero = jnp.zeros_like(a)
        stack = jnp.concatenate([a, b, a, b, c, a, zero, zero], axis=0).astype(BF16)
        both = mm(w6[...], stack)
        u, u_d = both[:, :TILE], both[:, TILE:]
        gate = 1.0 / (1.0 + jnp.exp(-u))
        hidden = u * gate
        slope = gate + hidden * (1.0 - gate)
        env, env_d = get_row(geo_d, 13, step), get_row(geo_d, 14, step)
        g = jnp.concatenate([env * hidden, env_d * hidden + env * (slope * u_d)], axis=1)
        hi, lo = split2(g)
        radial = mm(w3[...], jnp.concatenate([hi, lo, hi], axis=0))
        r_s[:, span(step)] = radial[:, :TILE]
        rp_s[:, span(step)] = radial[:, TILE:]

    loop(0, STEPS, radial_step, UNROLL_RADIAL)

    def messages(step, signs, features):
        radial = r_s[:, span(step)]
        for degree in range(3):
            product = radial[degree * CH : (degree + 1) * CH] * features
            for q in range(9):
                if DEGREE[q] != degree:
                    continue
                shape = get_row(geo_d, q, step)
                hi, lo = split2((shape * product) if signs[q] > 0 else (-shape * product))
                m_s[q * CH : (q + 1) * CH, 0:TILE] = hi
                m_s[q * CH : (q + 1) * CH, TILE : 2 * TILE] = lo

    s2[...] = jnp.zeros_like(s2)

    def other_step(step):
        messages(step, PARITY, fa_s[:, span(step)])
        table = oh2[0:EXT, span(step)]
        s2[...] += mm(jnp.concatenate([table, table], axis=1), m_s[...], NT)

    loop(0, STEPS, other_step, UNROLL_SUMS)

    c0 = push(4, s2.at[pl.ds(2 * OWN, GY)], rsy.at[pl.ds(GY, GY)], y_low)
    c1 = push(5, s2.at[pl.ds(2 * OWN + GY, GY)], rsy.at[pl.ds(0, GY)], y_high)

    s1[...] = jnp.zeros_like(s1)

    def own_sum_step(step):
        messages(step, (1.0,) * 9, fb_s[:, span(step)])
        table = oh1[:, span(step)]
        s1[...] += mm(m_s[...], jnp.concatenate([table, table], axis=1), NT)

    loop(0, STEPS // 2, own_sum_step, UNROLL_SUMS)
    settle(c0, c1)
    if comm:
        hi, lo = split2(rsy[...])
        s2[0 : 2 * OWN, :] += mm(ohy_t[:, 0 : 2 * GY], hi) + mm(ohy_t[:, 0 : 2 * GY], lo)
    c0 = push(6, s2.at[pl.ds(OWN, GX)], rsx.at[pl.ds(GX, GX)], x_low)
    c1 = push(7, s2.at[pl.ds(OWN + GX, GX)], rsx.at[pl.ds(0, GX)], x_high)
    loop(STEPS // 2, STEPS, own_sum_step, UNROLL_SUMS)
    settle(c0, c1)
    sums_t = s2[0:OWN, :]
    if comm:
        hi, lo = split2(rsx[...])
        sums_t = sums_t + mm(ohx_t, hi) + mm(ohx_t, lo)

    sums = s1[...] + sums_t.T
    squares = [sums[q * CH : (q + 1) * CH] * sums[q * CH : (q + 1) * CH] for q in range(9)]
    invariant = jnp.concatenate(
        [
            squares[0],
            squares[1] + squares[2] + squares[3],
            squares[4] + squares[5] + squares[6] + squares[7] + squares[8],
        ],
        axis=0,
    )
    mixed = mm(mix_ref[...], invariant, precision=HIGHEST) + feat_ref[...].astype(F32)
    gate = 1.0 / (1.0 + jnp.exp(-mixed))
    diagonal = iota((CH, CH), 0) == iota((CH, CH), 1)
    weight = jnp.sum(jnp.where(diagonal, outw_ref[...], 0.0), axis=1, keepdims=True)
    energy = jnp.sum(weight * (mixed * gate), axis=0, keepdims=True)
    kind = spec_ref[...]
    shift = jnp.zeros_like(energy)
    for k in range(5):
        shift = jnp.where(kind == k, se_ref[k], shift)
    energy_ref[...] = energy + shift
    d_mixed = weight * (gate * (1.0 + mixed * (1.0 - gate)))
    d_inv = 2.0 * mm(mix_ref[...].T, d_mixed, precision=HIGHEST)
    gext[...] = jnp.zeros_like(gext)
    for q in range(9):
        at = slice(q * CH, (q + 1) * CH)
        gradient = sums[at] * d_inv[DEGREE[q] * CH : (DEGREE[q] + 1) * CH]
        hi, lo = split2(gradient)
        gown[at, 0:OWN] = hi
        gown[at, OWN : 2 * OWN] = lo
        hi, lo = split2(PARITY[q] * gradient)
        gext[at, 0:OWN] = hi
        gext[at, EXT_PAD : EXT_PAD + OWN] = lo

    def own_rows(table):
        return mm(table, gext[:, 0:OWN], NT) + mm(table, gext[:, EXT_PAD : EXT_PAD + OWN], NT)

    sgx[...] = own_rows(ohx)
    c0 = push(8, sgx.at[pl.ds(0, GX)], rgx.at[pl.ds(GX, GX)], x_low)
    c1 = push(9, sgx.at[pl.ds(GX, GX)], rgx.at[pl.ds(0, GX)], x_high)
    outgoing_y = own_rows(ohy[0 : 2 * GY, 0:OWN])

    def store_ghosts(rows, start):
        hi, lo = split2(rows.T)
        count_here = rows.shape[0]
        gext[:, start : start + count_here] = hi
        gext[:, EXT_PAD + start : EXT_PAD + start + count_here] = lo

    def contract(step, gathered, features, target):
        along = None
        for degree in range(3):
            part = slice(degree * CH, (degree + 1) * CH)
            radial = r_s[part, span(step)] * features
            slope = rp_s[part, span(step)] * features
            total = None
            for q in range(9):
                if DEGREE[q] != degree:
                    continue
                here = gathered[q * CH : (q + 1) * CH]
                put_row(target, q, step, jnp.sum(radial * here, axis=0, keepdims=True))
                term = get_row(geo_d, q, step) * here
                total = term if total is None else total + term
            along = slope * total if along is None else along + slope * total
        put_row(target, 9, step, jnp.sum(along, axis=0, keepdims=True))

    def own_step(step):
        table = oh1[:, span(step)]
        gathered = mm(gown[...], jnp.concatenate([table, table], axis=0))
        contract(step, gathered, fb_s[:, span(step)], z_own)

    loop(0, 8, own_step, UNROLL_BACK)
    settle(c0, c1)
    if comm:
        hi, lo = split2(rgx[...])
        table = ohy[0 : 2 * GY, OWN : 2 * OWN]
        sgy[...] = outgoing_y + mm(table, hi) + mm(table, lo)
    c0 = push(10, sgy.at[pl.ds(0, GY)], rgy.at[pl.ds(GY, GY)], y_low)
    c1 = push(11, sgy.at[pl.ds(GY, GY)], rgy.at[pl.ds(0, GY)], y_high)
    if comm:
        store_ghosts(rgx[...], OWN)
    loop(8, STEPS, own_step, UNROLL_BACK)
    settle(c0, c1)
    if comm:
        store_ghosts(rgy[...], 2 * OWN)

    def ext_step(step):
        table = oh2[:, span(step)]
        gathered = mm(gext[...], jnp.concatenate([table, table], axis=0))
        contract(step, gathered, fa_s[:, span(step)], z_ext)

    loop(0, STEPS, ext_step, UNROLL_BACK)

    zs = [dense(z_own, q) + dense(z_ext, q) for q in range(10)]
    nx, ny, nz, inv = [dense(geo_d, number) for number in range(9, 13)]
    factor = SCALE * inv
    gx = factor * (S3 * zs[1] + S15 * (ny * zs[4] + nz * zs[7] + nx * zs[8]))
    gy = factor * (S3 * zs[2] + S15 * (nx * zs[4] + nz * zs[5] - ny * zs[8]))
    gz = factor * (S3 * zs[3] + S15 * (ny * zs[5] + nx * zs[7]) + (3.0 * S5) * (nz * zs[6]))
    along = zs[9] - (gx * nx + gy * ny + gz * nz)
    pull_d[...] = jnp.zeros_like(pull_d)
    for number, value in enumerate([gx + along * nx, gy + along * ny, gz + along * nz]):
        pull_d[number * DENSE : (number + 1) * DENSE, :] = value
    for step in range(STEPS):
        pulled = get_eight(pull_d, step)
        hi = pulled.astype(BF16).astype(F32)
        pieces_s[:, step * TILE : (step + 1) * TILE] = jnp.concatenate(
            [hi, pulled - hi], axis=0
        ).astype(BF16)
    at_first = mm(oh1[...], pieces_s[...], NT)
    at_second = mm(oh2[...], pieces_s[...], NT)

    def home(rows8, table):
        a, b, c = split3(rows8)
        out = mm(jnp.concatenate([a, b, c, jnp.zeros_like(a)], axis=0).astype(BF16), table)
        return out[0:8] + out[8:16] + out[16:24]

    at_first, at_second = at_first.T, -at_second.T
    at_first = at_first[0:8] + at_first[8:16]
    total = at_second[0:8] + at_second[8:16]
    send_f[0] = total[:, 2 * OWN : 3 * OWN]
    c0 = push(12, send_f.at[0], recv_f.at[1], y_low)
    c1 = push(13, send_f.at[0], recv_f.at[0], y_high)
    settle(c0, c1)
    near = jnp.concatenate([total[:, 0:OWN] + at_first, total[:, OWN : 2 * OWN]], axis=1)
    if comm:
        near = near + home(fold_y(recv_f[0], recv_f[1]), ohy)
    send_f[1] = near[:, OWN : 2 * OWN]
    c0 = push(14, send_f.at[1], recv_f.at[3], x_low)
    c1 = push(15, send_f.at[1], recv_f.at[2], x_high)
    settle(c0, c1)
    own = near[:, 0:OWN]
    if comm:
        own = own + home(fold_x(recv_f[2], recv_f[3]), ohx)
    force_ref[...] = own[0:3]


def run(args, n_gx, n_gy, comm=True):
    (
        positions,
        features,
        species,
        edge_list,
        edge_count,
        send_list_x,
        send_list_y,
        radial_in,
        radial_out,
        mix_weight,
        out_weight,
        species_energy,
    ) = args
    vmem = pl.BlockSpec(memory_space=pltpu.VMEM)
    smem = pl.BlockSpec(memory_space=pltpu.SMEM)
    scratch = [
        pltpu.VMEM((8, OWN), F32),
        pltpu.VMEM((1, OWN), jnp.int32),
        pltpu.VMEM((OWN, SLOTS), BF16),
        pltpu.VMEM((EXT_PAD, SLOTS), BF16),
        pltpu.VMEM((2, CH + 8, OWN), F32),
        pltpu.VMEM((4, CH + 8, OWN), F32),
        pltpu.VMEM((CH + 32, EXT_PAD), BF16),
        pltpu.VMEM((8, SLOTS), F32),
        pltpu.VMEM((3 * DENSE, OWN), F32),
        pltpu.VMEM((8 * DENSE, OWN), F32),
        pltpu.VMEM((8 * DENSE, OWN), F32),
        pltpu.VMEM((16 * DENSE, OWN), F32),
        pltpu.VMEM((8 * DENSE, OWN), F32),
        pltpu.VMEM((CH, SLOTS), F32),
        pltpu.VMEM((CH, SLOTS), F32),
        pltpu.VMEM((3 * CH, SLOTS), F32),
        pltpu.VMEM((3 * CH, SLOTS), F32),
        pltpu.VMEM((3 * CH, 3 * CH), BF16),
        pltpu.VMEM((CH, 64), BF16),
        pltpu.VMEM((ROWS, 2 * TILE), BF16),
        pltpu.VMEM((ROWS, OWN), F32),
        pltpu.VMEM((EXT, ROWS), F32),
        pltpu.VMEM((2 * GY, ROWS), F32),
        pltpu.VMEM((2 * GX, ROWS), F32),
        pltpu.VMEM((ROWS, 2 * OWN), BF16),
        pltpu.VMEM((ROWS, 2 * EXT_PAD), BF16),
        pltpu.VMEM((2 * GX, ROWS), F32),
        pltpu.VMEM((2 * GX, ROWS), F32),
        pltpu.VMEM((2 * GY, ROWS), F32),
        pltpu.VMEM((2 * GY, ROWS), F32),
        pltpu.VMEM((10 * DENSE, OWN), F32),
        pltpu.VMEM((10 * DENSE, OWN), F32),
        pltpu.VMEM((16, SLOTS), BF16),
        pltpu.VMEM((2, 8, OWN), F32),
        pltpu.VMEM((4, 8, OWN), F32),
        pltpu.SemaphoreType.DMA((16,)),
        pltpu.SemaphoreType.DMA((16,)),
    ]
    params = {"collective_id": 0, "has_side_effects": True} if comm else {}
    energies, forces = pl.pallas_call(
        functools.partial(body, comm, n_gx, n_gy),
        out_shape=(
            jax.ShapeDtypeStruct((1, OWN), F32),
            jax.ShapeDtypeStruct((3, OWN), F32),
        ),
        in_specs=[vmem, vmem, vmem, vmem, smem, vmem, vmem, vmem, vmem, vmem, vmem, smem],
        out_specs=(vmem, vmem),
        scratch_shapes=scratch,
        compiler_params=pltpu.CompilerParams(vmem_limit_bytes=60 * 1024 * 1024, **params),
        name="layer",
    )(
        positions,
        features,
        species.reshape(1, -1),
        edge_list,
        edge_count,
        send_list_x.reshape(1, -1),
        send_list_y.reshape(1, -1),
        radial_in.T,
        radial_out.T,
        mix_weight,
        out_weight.reshape(1, -1),
        species_energy,
    )
    return energies.reshape(-1), forces


def solution(mesh):
    n_gx, n_gy = mesh.shape["gx"], mesh.shape["gy"]
    both = ("gx", "gy")
    placed = (
        P(None, both),
        P(None, both),
        P(both),
        P(None, both),
        P(both),
        P(both),
        P(both),
        P(),
        P(),
        P(),
        P(),
        P(),
    )
    return jax.shard_map(
        lambda *args: run(args, n_gx, n_gy),
        mesh=mesh,
        in_specs=placed,
        out_specs=(P(both), P(None, both)),
        check_vma=False,
    )
```

```python
import functools
import math

import jax
import jax.numpy as jnp
from jax import lax
from jax.experimental import pallas as pl
from jax.experimental.pallas import tpu as pltpu
from jax.sharding import PartitionSpec as P

MESH = pl.DeviceIdType.MESH
F32 = jnp.float32
BF16 = jnp.bfloat16
HIGHEST = lax.Precision.HIGHEST

CH = 64
OWN = 128
GX = 64
GY = 32
EXT = 320
EXT_PAD = 384
TILE = 256
STEPS = 13
SLOTS = TILE * STEPS
ROWS = 9 * CH
DENSE = 32

CUTOFF = 5.0
SCALE = 0.3
S3 = math.sqrt(3.0)
S5 = math.sqrt(5.0)
S15 = math.sqrt(15.0)
DEGREE = (0, 1, 1, 1, 2, 2, 2, 2, 2)
PARITY = (1.0, -1.0, -1.0, -1.0, 1.0, 1.0, 1.0, 1.0, 1.0)

UNROLL_GATHER = True
UNROLL_RADIAL = True
UNROLL_SUMS = True
UNROLL_BACK = True

NN = (((1,), (0,)), ((), ()))
NT = (((1,), (1,)), ((), ()))


def mm(a, b, dims=NN, precision=None):
    return lax.dot_general(a, b, dims, precision=precision, preferred_element_type=F32)


def split2(x):
    hi = x.astype(BF16)
    return hi, (x - hi.astype(F32)).astype(BF16)


def split3(x):
    a = x.astype(BF16).astype(F32)
    b = (x - a).astype(BF16).astype(F32)
    return a, b, (x - a) - b


def iota(shape, dim):
    return lax.broadcasted_iota(jnp.int32, shape, dim)


def onehot(cond):
    return jnp.where(cond, 1.0, 0.0)


def sin_cos(arg):
    k = jnp.floor(arg * (1.0 / math.pi) + 0.5)
    r = (arg - k * 3.140625) - k * (math.pi - 3.140625)
    sign = 1.0 - 2.0 * (k - 2.0 * jnp.floor(k * 0.5))
    r2 = r * r
    s = 1.0 / 6227020800.0
    for c in (-1.0 / 39916800, 1.0 / 362880, -1.0 / 5040, 1.0 / 120, -1.0 / 6, 1.0):
        s = s * r2 + c
    q = -1.0 / 87178291200.0
    for c in (1.0 / 479001600, -1.0 / 3628800, 1.0 / 40320, -1.0 / 720, 1.0 / 24, -0.5, 1.0):
        q = q * r2 + c
    return sign * (s * r), sign * q


def body(
    comm,
    n_gx,
    n_gy,
    pos_ref,
    feat_ref,
    spec_ref,
    edge_ref,
    cnt_ref,
    slx_ref,
    sly_ref,
    win_ref,
    wout_ref,
    mix_ref,
    outw_ref,
    se_ref,
    energy_ref,
    force_ref,
    pos8,
    slyp,
    oh1,
    oh2,
    send_a,
    recv_a,
    ext_l,
    pa_s,
    rel_d,
    bes_d,
    slope_d,
    geo_d,
    pull_d,
    fa_s,
    fb_s,
    r_s,
    rp_s,
    w3,
    w6,
    m_s,
    s1,
    s2,
    rsy,
    rsx,
    gown,
    gext,
    sgx,
    rgx,
    sgy,
    rgy,
    z_own,
    z_ext,
    pieces_s,
    send_f,
    recv_f,
    send_sem,
    recv_sem,
):
    if comm:
        ix = lax.axis_index("gx")
        iy = lax.axis_index("gy")
        x_low = (lax.rem(ix + n_gx - 1, n_gx), iy)
        x_high = (lax.rem(ix + 1, n_gx), iy)
        y_low = (ix, lax.rem(iy + n_gy - 1, n_gy))
        y_high = (ix, lax.rem(iy + 1, n_gy))
        barrier = pltpu.get_barrier_semaphore()
        for device in (x_low, x_high, y_low, y_high):
            pl.semaphore_signal(barrier, inc=1, device_id=device, device_id_type=MESH)
    else:
        x_low = x_high = y_low = y_high = None

    def push(number, src, dst, device):
        if not comm:
            return None
        copy = pltpu.make_async_remote_copy(
            src_ref=src,
            dst_ref=dst,
            send_sem=send_sem.at[number],
            recv_sem=recv_sem.at[number],
            device_id=device,
            device_id_type=MESH,
        )
        copy.start()
        return copy

    def settle(*copies):
        for copy in copies:
            if copy is not None:
                copy.wait()

    lane = iota((1, OWN), 1)

    slyp[...] = jnp.full_like(slyp, -1)
    slyp[:, 0 : 2 * GY] = sly_ref[...]
    ohx_t32 = onehot(iota((OWN, OWN), 0) == slx_ref[...])
    ohy_t32 = onehot(iota((2 * OWN, OWN), 0) == slyp[...])
    ohx_t = ohx_t32.astype(BF16)
    ohy_t = ohy_t32.astype(BF16)
    ohx = ohx_t32.T.astype(BF16)
    ohy = ohy_t32.T.astype(BF16)

    def pack(rows72):
        a, b, c = split3(rows72[CH : CH + 8])
        pieces = jnp.concatenate([a, b, c, jnp.zeros_like(a)], axis=0).astype(BF16)
        return jnp.concatenate([rows72[:CH].astype(BF16), pieces], axis=0)

    def unpack(rows96):
        return (rows96[CH : CH + 8] + rows96[CH + 8 : CH + 16]) + rows96[CH + 16 : CH + 24]

    def fold_x(low, high):
        return jnp.where(lane < GX, pltpu.roll(low, GX, 1), pltpu.roll(high, GX, 1))

    def fold_y(low, high):
        picked = jnp.where(lane < GY, pltpu.roll(low, OWN - GY, 1), pltpu.roll(high, GY, 1))
        return jnp.where(lane < 2 * GY, picked, 0.0)

    pos8[...] = jnp.zeros_like(pos8)
    pos8[0:3, :] = pos_ref[...]
    own_l = pack(jnp.concatenate([feat_ref[...].astype(F32), pos8[...]], axis=0))
    ext_l[:, 0:OWN] = own_l
    picked = mm(own_l, ohx_t)
    send_a[0, 0:CH, :] = picked[0:CH]
    send_a[0, CH : CH + 8, :] = unpack(picked)
    if comm:
        pl.semaphore_wait(barrier, 4)
    c0 = push(0, send_a.at[0], recv_a.at[1], x_low)
    c1 = push(1, send_a.at[0], recv_a.at[0], x_high)

    hi, lo = split2(wout_ref[...])
    hi, lo = hi.astype(F32), lo.astype(F32)
    w3[...] = jnp.concatenate([hi, hi, lo], axis=0).T.astype(BF16)
    a, b, c = split3(win_ref[...])
    zero = jnp.zeros_like(a)
    w6[...] = jnp.concatenate([a, a, b, b, a, c, zero, zero], axis=0).T.astype(BF16)
    count = cnt_ref[0]

    def table_step(step, carry):
        at = pl.ds(pl.multiple_of(step * TILE, TILE), TILE)
        live = iota((1, TILE), 1) + step * TILE < count
        first = jnp.where(live, edge_ref[0:1, at], -1)
        second = jnp.where(live, edge_ref[1:2, at], -1)
        table1 = onehot(iota((OWN, TILE), 0) == first).astype(BF16)
        oh1[:, at] = table1
        oh2[:, at] = onehot(iota((EXT_PAD, TILE), 0) == second).astype(BF16)
        got = mm(ext_l[:, 0:OWN], table1)
        fa_s[:, at] = got[0:CH]
        pa_s[:, at] = unpack(got)
        return carry

    lax.fori_loop(0, STEPS, table_step, 0)

    settle(c0, c1)
    if comm:
        section = pack(fold_x(recv_a[0], recv_a[1]))
    else:
        section = own_l
    ext_l[:, OWN : 2 * OWN] = section
    picked = mm(own_l, ohy_t[0:OWN]) + mm(section, ohy_t[OWN : 2 * OWN])
    send_a[1, 0:CH, :] = picked[0:CH]
    send_a[1, CH : CH + 8, :] = unpack(picked)
    c0 = push(2, send_a.at[1], recv_a.at[3], y_low)
    c1 = push(3, send_a.at[1], recv_a.at[2], y_high)
    settle(c0, c1)
    if comm:
        ext_l[:, 2 * OWN : 3 * OWN] = pack(fold_y(recv_a[2], recv_a[3]))
    else:
        ext_l[:, 2 * OWN : 3 * OWN] = jnp.where(lane < 2 * GY, own_l, 0.0)

    def span(step):
        return pl.ds(pl.multiple_of(step * TILE, TILE), TILE)

    def loop(start, stop, step_fn, unroll):
        def one(step, carry):
            step_fn(step)
            return carry

        lax.fori_loop(start, stop, one, 0, unroll=unroll)

    def halves(value):
        return value[:, 0:OWN], value[:, OWN:TILE]

    def get_row(ref, number, step):
        at = number * DENSE + 2 * step
        return jnp.concatenate([ref[pl.ds(at, 1), :], ref[pl.ds(at + 1, 1), :]], axis=1)

    def put_row(ref, number, step, value):
        at = number * DENSE + 2 * step
        low, high = halves(value)
        ref[pl.ds(at, 1), :] = low
        ref[pl.ds(at + 1, 1), :] = high

    def get_eight(ref, step):
        at = 2 * step
        return jnp.concatenate(
            [ref[pl.ds(at, 8, stride=DENSE), :], ref[pl.ds(at + 1, 8, stride=DENSE), :]], axis=1
        )

    def dense(ref, number):
        return ref[number * DENSE : (number + 1) * DENSE, :]

    rel_d[...] = jnp.full_like(rel_d, 2.0)

    def gather_step(step):
        got = mm(ext_l[...], oh2[:, span(step)])
        fb_s[:, span(step)] = got[0:CH]
        relative = unpack(got) - pa_s[:, span(step)]
        for number in range(3):
            put_row(rel_d, number, step, relative[number : number + 1])

    loop(0, STEPS, gather_step, UNROLL_GATHER)

    live = iota((DENSE, OWN), 0) * OWN + iota((DENSE, OWN), 1) < count
    rx = jnp.where(live, dense(rel_d, 0), 2.0)
    ry = jnp.where(live, dense(rel_d, 1), 0.0)
    rz = jnp.where(live, dense(rel_d, 2), 0.0)
    d = jnp.sqrt(rx * rx + ry * ry + rz * rz)
    inv = 1.0 / d
    x, y, z = rx * inv, ry * inv, rz * inv
    scaled = d * (1.0 / CUTOFF)
    left = 1.0 - scaled * scaled
    inside = d < CUTOFF
    values = [
        jnp.full_like(x, SCALE),
        (SCALE * S3) * x,
        (SCALE * S3) * y,
        (SCALE * S3) * z,
        (SCALE * S15) * (x * y),
        (SCALE * S15) * (y * z),
        (SCALE * 0.5 * S5) * (3.0 * z * z - 1.0),
        (SCALE * S15) * (x * z),
        (SCALE * 0.5 * S15) * (x * x - y * y),
        x,
        y,
        z,
        inv,
        jnp.where(inside, left * left, 0.0),
        jnp.where(inside, (-4.0 / CUTOFF) * scaled * left, 0.0),
    ]
    for number, value in enumerate(values):
        geo_d[number * DENSE : (number + 1) * DENSE, :] = value
    sine, cosine = sin_cos(d * (math.pi / CUTOFF))
    twice = 2.0 * cosine
    sine_last, cosine_last = jnp.zeros_like(sine), jnp.ones_like(sine)
    root = math.sqrt(2.0 / CUTOFF)
    for number in range(8):
        bessel = root * sine * inv
        bes_d[number * DENSE : (number + 1) * DENSE, :] = bessel
        slope_d[number * DENSE : (number + 1) * DENSE, :] = (
            (root * (math.pi / CUTOFF) * (number + 1)) * cosine - bessel
        ) * inv
        sine, sine_last = twice * sine - sine_last, sine
        cosine, cosine_last = twice * cosine - cosine_last, cosine

    def radial_step(step):
        basis = jnp.concatenate([get_eight(bes_d, step), get_eight(slope_d, step)], axis=1)
        a, b, c = split3(basis)
        zero = jnp.zeros_like(a)
        stack = jnp.concatenate([a, b, a, b, c, a, zero, zero], axis=0).astype(BF16)
        both = mm(w6[...], stack)
        u, u_d = both[:, :TILE], both[:, TILE:]
        gate = 1.0 / (1.0 + jnp.exp(-u))
        hidden = u * gate
        slope = gate + hidden * (1.0 - gate)
        env, env_d = get_row(geo_d, 13, step), get_row(geo_d, 14, step)
        g = jnp.concatenate([env * hidden, env_d * hidden + env * (slope * u_d)], axis=1)
        hi, lo = split2(g)
        radial = mm(w3[...], jnp.concatenate([hi, lo, hi], axis=0))
        r_s[:, span(step)] = radial[:, :TILE]
        rp_s[:, span(step)] = radial[:, TILE:]

    loop(0, STEPS, radial_step, UNROLL_RADIAL)

    def messages(step, signs, features):
        radial = r_s[:, span(step)]
        for degree in range(3):
            product = radial[degree * CH : (degree + 1) * CH] * features
            for q in range(9):
                if DEGREE[q] != degree:
                    continue
                shape = get_row(geo_d, q, step)
                hi, lo = split2((shape * product) if signs[q] > 0 else (-shape * product))
                m_s[q * CH : (q + 1) * CH, 0:TILE] = hi
                m_s[q * CH : (q + 1) * CH, TILE : 2 * TILE] = lo

    s2[...] = jnp.zeros_like(s2)

    def other_step(step):
        messages(step, PARITY, fa_s[:, span(step)])
        table = oh2[0:EXT, span(step)]
        s2[...] += mm(jnp.concatenate([table, table], axis=1), m_s[...], NT)

    loop(0, STEPS, other_step, UNROLL_SUMS)

    c0 = push(4, s2.at[pl.ds(2 * OWN, GY)], rsy.at[pl.ds(GY, GY)], y_low)
    c1 = push(5, s2.at[pl.ds(2 * OWN + GY, GY)], rsy.at[pl.ds(0, GY)], y_high)

    s1[...] = jnp.zeros_like(s1)

    def own_sum_step(step):
        messages(step, (1.0,) * 9, fb_s[:, span(step)])
        table = oh1[:, span(step)]
        s1[...] += mm(m_s[...], jnp.concatenate([table, table], axis=1), NT)

    loop(0, STEPS // 2, own_sum_step, UNROLL_SUMS)
    settle(c0, c1)
    if comm:
        hi, lo = split2(rsy[...])
        s2[0 : 2 * OWN, :] += mm(ohy_t[:, 0 : 2 * GY], hi) + mm(ohy_t[:, 0 : 2 * GY], lo)
    c0 = push(6, s2.at[pl.ds(OWN, GX)], rsx.at[pl.ds(GX, GX)], x_low)
    c1 = push(7, s2.at[pl.ds(OWN + GX, GX)], rsx.at[pl.ds(0, GX)], x_high)
    loop(STEPS // 2, STEPS, own_sum_step, UNROLL_SUMS)
    settle(c0, c1)
    sums_t = s2[0:OWN, :]
    if comm:
        hi, lo = split2(rsx[...])
        sums_t = sums_t + mm(ohx_t, hi) + mm(ohx_t, lo)

    sums = s1[...] + sums_t.T
    squares = [sums[q * CH : (q + 1) * CH] * sums[q * CH : (q + 1) * CH] for q in range(9)]
    invariant = jnp.concatenate(
        [
            squares[0],
            squares[1] + squares[2] + squares[3],
            squares[4] + squares[5] + squares[6] + squares[7] + squares[8],
        ],
        axis=0,
    )
    mixed = mm(mix_ref[...], invariant, precision=HIGHEST) + feat_ref[...].astype(F32)
    gate = 1.0 / (1.0 + jnp.exp(-mixed))
    diagonal = iota((CH, CH), 0) == iota((CH, CH), 1)
    weight = jnp.sum(jnp.where(diagonal, outw_ref[...], 0.0), axis=1, keepdims=True)
    energy = jnp.sum(weight * (mixed * gate), axis=0, keepdims=True)
    kind = spec_ref[...]
    shift = jnp.zeros_like(energy)
    for k in range(5):
        shift = jnp.where(kind == k, se_ref[k], shift)
    energy_ref[...] = energy + shift
    d_mixed = weight * (gate * (1.0 + mixed * (1.0 - gate)))
    d_inv = 2.0 * mm(mix_ref[...].T, d_mixed, precision=HIGHEST)
    gext[...] = jnp.zeros_like(gext)
    for q in range(9):
        at = slice(q * CH, (q + 1) * CH)
        gradient = sums[at] * d_inv[DEGREE[q] * CH : (DEGREE[q] + 1) * CH]
        hi, lo = split2(gradient)
        gown[at, 0:OWN] = hi
        gown[at, OWN : 2 * OWN] = lo
        hi, lo = split2(PARITY[q] * gradient)
        gext[at, 0:OWN] = hi
        gext[at, EXT_PAD : EXT_PAD + OWN] = lo

    def own_rows(table):
        return mm(table, gext[:, 0:OWN], NT) + mm(table, gext[:, EXT_PAD : EXT_PAD + OWN], NT)

    sgx[...] = own_rows(ohx)
    c0 = push(8, sgx.at[pl.ds(0, GX)], rgx.at[pl.ds(GX, GX)], x_low)
    c1 = push(9, sgx.at[pl.ds(GX, GX)], rgx.at[pl.ds(0, GX)], x_high)
    outgoing_y = own_rows(ohy[0 : 2 * GY, 0:OWN])

    def store_ghosts(rows, start):
        hi, lo = split2(rows.T)
        count_here = rows.shape[0]
        gext[:, start : start + count_here] = hi
        gext[:, EXT_PAD + start : EXT_PAD + start + count_here] = lo

    def contract(step, gathered, features, target):
        along = None
        for degree in range(3):
            part = slice(degree * CH, (degree + 1) * CH)
            radial = r_s[part, span(step)] * features
            slope = rp_s[part, span(step)] * features
            total = None
            for q in range(9):
                if DEGREE[q] != degree:
                    continue
                here = gathered[q * CH : (q + 1) * CH]
                put_row(target, q, step, jnp.sum(radial * here, axis=0, keepdims=True))
                term = get_row(geo_d, q, step) * here
                total = term if total is None else total + term
            along = slope * total if along is None else along + slope * total
        put_row(target, 9, step, jnp.sum(along, axis=0, keepdims=True))

    def own_step(step):
        table = oh1[:, span(step)]
        gathered = mm(gown[...], jnp.concatenate([table, table], axis=0))
        contract(step, gathered, fb_s[:, span(step)], z_own)

    loop(0, 8, own_step, UNROLL_BACK)
    settle(c0, c1)
    if comm:
        hi, lo = split2(rgx[...])
        table = ohy[0 : 2 * GY, OWN : 2 * OWN]
        sgy[...] = outgoing_y + mm(table, hi) + mm(table, lo)
    c0 = push(10, sgy.at[pl.ds(0, GY)], rgy.at[pl.ds(GY, GY)], y_low)
    c1 = push(11, sgy.at[pl.ds(GY, GY)], rgy.at[pl.ds(0, GY)], y_high)
    if comm:
        store_ghosts(rgx[...], OWN)
    loop(8, STEPS, own_step, UNROLL_BACK)
    settle(c0, c1)
    if comm:
        store_ghosts(rgy[...], 2 * OWN)

    def ext_step(step):
        table = oh2[:, span(step)]
        gathered = mm(gext[...], jnp.concatenate([table, table], axis=0))
        contract(step, gathered, fa_s[:, span(step)], z_ext)

    loop(0, STEPS, ext_step, UNROLL_BACK)

    zs = [dense(z_own, q) + dense(z_ext, q) for q in range(10)]
    nx, ny, nz, inv = [dense(geo_d, number) for number in range(9, 13)]
    factor = SCALE * inv
    gx = factor * (S3 * zs[1] + S15 * (ny * zs[4] + nz * zs[7] + nx * zs[8]))
    gy = factor * (S3 * zs[2] + S15 * (nx * zs[4] + nz * zs[5] - ny * zs[8]))
    gz = factor * (S3 * zs[3] + S15 * (ny * zs[5] + nx * zs[7]) + (3.0 * S5) * (nz * zs[6]))
    along = zs[9] - (gx * nx + gy * ny + gz * nz)
    pull_d[...] = jnp.zeros_like(pull_d)
    for number, value in enumerate([gx + along * nx, gy + along * ny, gz + along * nz]):
        pull_d[number * DENSE : (number + 1) * DENSE, :] = value
    for step in range(STEPS):
        pulled = get_eight(pull_d, step)
        hi = pulled.astype(BF16).astype(F32)
        pieces_s[:, step * TILE : (step + 1) * TILE] = jnp.concatenate(
            [hi, pulled - hi], axis=0
        ).astype(BF16)
    at_first = mm(oh1[...], pieces_s[...], NT)
    at_second = mm(oh2[...], pieces_s[...], NT)

    def home(rows8, table):
        a, b, c = split3(rows8)
        out = mm(jnp.concatenate([a, b, c, jnp.zeros_like(a)], axis=0).astype(BF16), table)
        return out[0:8] + out[8:16] + out[16:24]

    at_first, at_second = at_first.T, -at_second.T
    at_first = at_first[0:8] + at_first[8:16]
    total = at_second[0:8] + at_second[8:16]
    send_f[0] = total[:, 2 * OWN : 3 * OWN]
    c0 = push(12, send_f.at[0], recv_f.at[1], y_low)
    c1 = push(13, send_f.at[0], recv_f.at[0], y_high)
    settle(c0, c1)
    near = jnp.concatenate([total[:, 0:OWN] + at_first, total[:, OWN : 2 * OWN]], axis=1)
    if comm:
        near = near + home(fold_y(recv_f[0], recv_f[1]), ohy)
    send_f[1] = near[:, OWN : 2 * OWN]
    c0 = push(14, send_f.at[1], recv_f.at[3], x_low)
    c1 = push(15, send_f.at[1], recv_f.at[2], x_high)
    settle(c0, c1)
    own = near[:, 0:OWN]
    if comm:
        own = own + home(fold_x(recv_f[2], recv_f[3]), ohx)
    force_ref[...] = own[0:3]


def run(args, n_gx, n_gy, comm=True):
    (
        positions,
        features,
        species,
        edge_list,
        edge_count,
        send_list_x,
        send_list_y,
        radial_in,
        radial_out,
        mix_weight,
        out_weight,
        species_energy,
    ) = args
    vmem = pl.BlockSpec(memory_space=pltpu.VMEM)
    smem = pl.BlockSpec(memory_space=pltpu.SMEM)
    scratch = [
        pltpu.VMEM((8, OWN), F32),
        pltpu.VMEM((1, OWN), jnp.int32),
        pltpu.VMEM((OWN, SLOTS), BF16),
        pltpu.VMEM((EXT_PAD, SLOTS), BF16),
        pltpu.VMEM((2, CH + 8, OWN), F32),
        pltpu.VMEM((4, CH + 8, OWN), F32),
        pltpu.VMEM((CH + 32, EXT_PAD), BF16),
        pltpu.VMEM((8, SLOTS), F32),
        pltpu.VMEM((3 * DENSE, OWN), F32),
        pltpu.VMEM((8 * DENSE, OWN), F32),
        pltpu.VMEM((8 * DENSE, OWN), F32),
        pltpu.VMEM((16 * DENSE, OWN), F32),
        pltpu.VMEM((8 * DENSE, OWN), F32),
        pltpu.VMEM((CH, SLOTS), F32),
        pltpu.VMEM((CH, SLOTS), F32),
        pltpu.VMEM((3 * CH, SLOTS), F32),
        pltpu.VMEM((3 * CH, SLOTS), F32),
        pltpu.VMEM((3 * CH, 3 * CH), BF16),
        pltpu.VMEM((CH, 64), BF16),
        pltpu.VMEM((ROWS, 2 * TILE), BF16),
        pltpu.VMEM((ROWS, OWN), F32),
        pltpu.VMEM((EXT, ROWS), F32),
        pltpu.VMEM((2 * GY, ROWS), F32),
        pltpu.VMEM((2 * GX, ROWS), F32),
        pltpu.VMEM((ROWS, 2 * OWN), BF16),
        pltpu.VMEM((ROWS, 2 * EXT_PAD), BF16),
        pltpu.VMEM((2 * GX, ROWS), F32),
        pltpu.VMEM((2 * GX, ROWS), F32),
        pltpu.VMEM((2 * GY, ROWS), F32),
        pltpu.VMEM((2 * GY, ROWS), F32),
        pltpu.VMEM((10 * DENSE, OWN), F32),
        pltpu.VMEM((10 * DENSE, OWN), F32),
        pltpu.VMEM((16, SLOTS), BF16),
        pltpu.VMEM((2, 8, OWN), F32),
        pltpu.VMEM((4, 8, OWN), F32),
        pltpu.SemaphoreType.DMA((16,)),
        pltpu.SemaphoreType.DMA((16,)),
    ]
    params = {"collective_id": 0, "has_side_effects": True} if comm else {}
    energies, forces = pl.pallas_call(
        functools.partial(body, comm, n_gx, n_gy),
        out_shape=(
            jax.ShapeDtypeStruct((1, OWN), F32),
            jax.ShapeDtypeStruct((3, OWN), F32),
        ),
        in_specs=[vmem, vmem, vmem, vmem, smem, vmem, vmem, vmem, vmem, vmem, vmem, smem],
        out_specs=(vmem, vmem),
        scratch_shapes=scratch,
        compiler_params=pltpu.CompilerParams(vmem_limit_bytes=60 * 1024 * 1024, **params),
        name="layer",
    )(
        positions,
        features,
        species.reshape(1, -1),
        edge_list,
        edge_count,
        send_list_x.reshape(1, -1),
        send_list_y.reshape(1, -1),
        radial_in.T,
        radial_out.T,
        mix_weight,
        out_weight.reshape(1, -1),
        species_energy,
    )
    return energies.reshape(-1), forces


def solution(mesh):
    n_gx, n_gy = mesh.shape["gx"], mesh.shape["gy"]
    both = ("gx", "gy")
    placed = (
        P(None, both),
        P(None, both),
        P(both),
        P(None, both),
        P(both),
        P(both),
        P(both),
        P(),
        P(),
        P(),
        P(),
        P(),
    )
    return jax.shard_map(
        lambda *args: run(args, n_gx, n_gy),
        mesh=mesh,
        in_specs=placed,
        out_specs=(P(both), P(None, both)),
        check_vma=False,
    )
```

```python
import functools
import math

import jax
import jax.numpy as jnp
from jax import lax
from jax.experimental import pallas as pl
from jax.experimental.pallas import tpu as pltpu
from jax.sharding import PartitionSpec as P

MESH = pl.DeviceIdType.MESH
F32 = jnp.float32
BF16 = jnp.bfloat16
HIGHEST = lax.Precision.HIGHEST

CH = 64
OWN = 128
GX = 64
GY = 32
EXT = 320
EXT_PAD = 384
TILE = 256
STEPS = 13
SLOTS = TILE * STEPS
ROWS = 9 * CH
DENSE = 32

CUTOFF = 5.0
SCALE = 0.3
S3 = math.sqrt(3.0)
S5 = math.sqrt(5.0)
S15 = math.sqrt(15.0)
DEGREE = (0, 1, 1, 1, 2, 2, 2, 2, 2)
GROUPS = (((2,), 256, 576), ((0, 1), 0, 256))
PARITY = (1.0, -1.0, -1.0, -1.0, 1.0, 1.0, 1.0, 1.0, 1.0)

UNROLL_GATHER = True
UNROLL_RADIAL = True
UNROLL_SUMS = True
UNROLL_BACK = True

NN = (((1,), (0,)), ((), ()))
NT = (((1,), (1,)), ((), ()))


def mm(a, b, dims=NN, precision=None):
    return lax.dot_general(a, b, dims, precision=precision, preferred_element_type=F32)


def split2(x):
    hi = x.astype(BF16)
    return hi, (x - hi.astype(F32)).astype(BF16)


def split3(x):
    a = x.astype(BF16).astype(F32)
    b = (x - a).astype(BF16).astype(F32)
    return a, b, (x - a) - b


def iota(shape, dim):
    return lax.broadcasted_iota(jnp.int32, shape, dim)


def onehot(cond):
    return jnp.where(cond, 1.0, 0.0)


def sin_cos(arg):
    k = jnp.floor(arg * (1.0 / math.pi) + 0.5)
    r = (arg - k * 3.140625) - k * (math.pi - 3.140625)
    sign = 1.0 - 2.0 * (k - 2.0 * jnp.floor(k * 0.5))
    r2 = r * r
    s = 1.0 / 6227020800.0
    for c in (-1.0 / 39916800, 1.0 / 362880, -1.0 / 5040, 1.0 / 120, -1.0 / 6, 1.0):
        s = s * r2 + c
    q = -1.0 / 87178291200.0
    for c in (1.0 / 479001600, -1.0 / 3628800, 1.0 / 40320, -1.0 / 720, 1.0 / 24, -0.5, 1.0):
        q = q * r2 + c
    return sign * (s * r), sign * q


def body(
    comm,
    n_gx,
    n_gy,
    pos_ref,
    feat_ref,
    spec_ref,
    edge_ref,
    cnt_ref,
    slx_ref,
    sly_ref,
    win_ref,
    wout_ref,
    mix_ref,
    outw_ref,
    se_ref,
    out_ref,
    pos8,
    slyp,
    oh1,
    oh2,
    send_x,
    recv_x,
    send_y,
    recv_y,
    ext_l,
    pa_s,
    rel_d,
    bes_d,
    slope_d,
    geo_d,
    pull_d,
    fa_s,
    fb_s,
    r_s,
    rp_s,
    w3,
    w6,
    m_s,
    m2_s,
    s1,
    s2a,
    s2b,
    rsya,
    rsyb,
    rsxa,
    rsxb,
    gown,
    gown2,
    gext,
    sgxa,
    sgxb,
    rgxa,
    rgxb,
    sgya,
    sgyb,
    rgya,
    rgyb,
    z_own,
    z_ext,
    pieces_s,
    send_f,
    recv_f,
    send_sem,
    recv_sem,
):
    s2, rsy, rsx = (s2a, s2b), (rsya, rsyb), (rsxa, rsxb)
    sgx, rgx, sgy, rgy = (sgxa, sgxb), (rgxa, rgxb), (sgya, sgyb), (rgya, rgyb)
    if comm:
        ix = lax.axis_index("gx")
        iy = lax.axis_index("gy")
        x_low = (lax.rem(ix + n_gx - 1, n_gx), iy)
        x_high = (lax.rem(ix + 1, n_gx), iy)
        y_low = (ix, lax.rem(iy + n_gy - 1, n_gy))
        y_high = (ix, lax.rem(iy + 1, n_gy))
        barrier = pltpu.get_barrier_semaphore()
        for device in (x_low, x_high, y_low, y_high):
            pl.semaphore_signal(barrier, inc=1, device_id=device, device_id_type=MESH)
    else:
        x_low = x_high = y_low = y_high = None

    def push(number, src, dst, device):
        if not comm:
            return None
        copy = pltpu.make_async_remote_copy(
            src_ref=src,
            dst_ref=dst,
            send_sem=send_sem.at[number],
            recv_sem=recv_sem.at[number],
            device_id=device,
            device_id_type=MESH,
        )
        copy.start()
        return copy

    def settle(*copies):
        for copy in copies:
            if copy is not None:
                copy.wait()

    lane = iota((1, OWN), 1)

    slyp[...] = jnp.full_like(slyp, -1)
    slyp[:, 0 : 2 * GY] = sly_ref[...]
    ohx_t32 = onehot(iota((OWN, OWN), 0) == slx_ref[...])
    ohy_t32 = onehot(iota((2 * OWN, OWN), 0) == slyp[...])
    ohx_t = ohx_t32.astype(BF16)
    ohy_t = ohy_t32.astype(BF16)
    ohx = ohx_t32.T.astype(BF16)
    ohy = ohy_t32.T.astype(BF16)

    def pack(rows72):
        a, b, c = split3(rows72[CH : CH + 8])
        pieces = jnp.concatenate([a, b, c, jnp.zeros_like(a)], axis=0).astype(BF16)
        return jnp.concatenate([rows72[:CH].astype(BF16), pieces], axis=0)

    def unpack(rows96):
        return (rows96[CH : CH + 8] + rows96[CH + 8 : CH + 16]) + rows96[CH + 16 : CH + 24]

    def fold_x(low, high):
        return jnp.where(lane < GX, pltpu.roll(low, GX, 1), pltpu.roll(high, GX, 1))

    def fold_y(low, high):
        picked = jnp.where(lane < GY, pltpu.roll(low, OWN - GY, 1), pltpu.roll(high, GY, 1))
        return jnp.where(lane < 2 * GY, picked, 0.0)

    pos8[...] = jnp.zeros_like(pos8)
    pos8[0:3, :] = pos_ref[...]
    own_l = pack(jnp.concatenate([feat_ref[...].astype(F32), pos8[...]], axis=0))
    ext_l[:, 0:OWN] = own_l
    picked = mm(own_l, ohx_t)
    half = CH // 2
    upper, lower = picked[0:half], picked[half:CH]
    near_low = lane < GX
    send_x[0, 0:half, :] = jnp.where(near_low, upper, pltpu.roll(lower, GX, 1))
    send_x[1, 0:half, :] = jnp.where(near_low, pltpu.roll(upper, GX, 1), lower)
    coordinates = unpack(picked)
    send_x[0, half:, :] = coordinates
    send_x[1, half:, :] = coordinates
    if comm:
        pl.semaphore_wait(barrier, 4)
    c0 = push(0, send_x.at[0], recv_x.at[1], x_low)
    c1 = push(1, send_x.at[1], recv_x.at[0], x_high)

    hi, lo = split2(wout_ref[...])
    hi, lo = hi.astype(F32), lo.astype(F32)
    w3[...] = jnp.concatenate([hi, hi, lo], axis=0).T.astype(BF16)
    a, b, c = split3(win_ref[...])
    zero = jnp.zeros_like(a)
    w6[...] = jnp.concatenate([a, a, b, b, a, c, zero, zero], axis=0).T.astype(BF16)
    count = cnt_ref[0]

    def table_step(step, carry):
        at = pl.ds(pl.multiple_of(step * TILE, TILE), TILE)
        live = iota((1, TILE), 1) + step * TILE < count
        first = jnp.where(live, edge_ref[0:1, at], -1)
        second = jnp.where(live, edge_ref[1:2, at], -1)
        table1 = onehot(iota((OWN, TILE), 0) == first).astype(BF16)
        oh1[:, at] = table1
        oh2[:, at] = onehot(iota((EXT_PAD, TILE), 0) == second).astype(BF16)
        got = mm(ext_l[:, 0:OWN], table1)
        fa_s[:, at] = got[0:CH]
        pa_s[:, at] = unpack(got)
        return carry

    lax.fori_loop(0, STEPS, table_step, 0)

    settle(c0, c1)
    if comm:
        low, high = recv_x[0], recv_x[1]
        turned_low, turned_high = pltpu.roll(low, GX, 1), pltpu.roll(high, GX, 1)
        upper = jnp.where(near_low, low[0:half], turned_high[0:half])
        lower = jnp.where(near_low, turned_low[0:half], high[0:half])
        coordinates = jnp.where(near_low, turned_low[half:], turned_high[half:])
        section = pack(jnp.concatenate([upper, lower, coordinates], axis=0))
    else:
        section = own_l
    ext_l[:, OWN : 2 * OWN] = section
    picked = mm(own_l, ohy_t[0:OWN]) + mm(section, ohy_t[OWN : 2 * OWN])
    send_y[0:CH, :] = picked[0:CH]
    send_y[CH : CH + 8, :] = unpack(picked)
    c0 = push(2, send_y, recv_y.at[1], y_low)
    c1 = push(3, send_y, recv_y.at[0], y_high)
    settle(c0, c1)
    if comm:
        ext_l[:, 2 * OWN : 3 * OWN] = pack(fold_y(recv_y[0], recv_y[1]))
    else:
        ext_l[:, 2 * OWN : 3 * OWN] = jnp.where(lane < 2 * GY, own_l, 0.0)

    def span(step):
        return pl.ds(pl.multiple_of(step * TILE, TILE), TILE)

    def loop(start, stop, step_fn, unroll):
        def one(step, carry):
            step_fn(step)
            return carry

        lax.fori_loop(start, stop, one, 0, unroll=unroll)

    def halves(value):
        return value[:, 0:OWN], value[:, OWN:TILE]

    def get_row(ref, number, step):
        at = number * DENSE + 2 * step
        return jnp.concatenate([ref[pl.ds(at, 1), :], ref[pl.ds(at + 1, 1), :]], axis=1)

    def put_row(ref, number, step, value):
        at = number * DENSE + 2 * step
        low, high = halves(value)
        ref[pl.ds(at, 1), :] = low
        ref[pl.ds(at + 1, 1), :] = high

    def get_eight(ref, step):
        at = 2 * step
        return jnp.concatenate(
            [ref[pl.ds(at, 8, stride=DENSE), :], ref[pl.ds(at + 1, 8, stride=DENSE), :]], axis=1
        )

    def dense(ref, number):
        return ref[number * DENSE : (number + 1) * DENSE, :]

    rel_d[...] = jnp.full_like(rel_d, 2.0)

    def gather_step(step):
        got = mm(ext_l[...], oh2[:, span(step)])
        fb_s[:, span(step)] = got[0:CH]
        relative = unpack(got) - pa_s[:, span(step)]
        for number in range(3):
            put_row(rel_d, number, step, relative[number : number + 1])

    loop(0, STEPS, gather_step, UNROLL_GATHER)

    live = iota((DENSE, OWN), 0) * OWN + iota((DENSE, OWN), 1) < count
    rx = jnp.where(live, dense(rel_d, 0), 2.0)
    ry = jnp.where(live, dense(rel_d, 1), 0.0)
    rz = jnp.where(live, dense(rel_d, 2), 0.0)
    d = jnp.sqrt(rx * rx + ry * ry + rz * rz)
    inv = 1.0 / d
    x, y, z = rx * inv, ry * inv, rz * inv
    scaled = d * (1.0 / CUTOFF)
    left = 1.0 - scaled * scaled
    inside = d < CUTOFF
    values = [
        jnp.full_like(x, SCALE),
        (SCALE * S3) * x,
        (SCALE * S3) * y,
        (SCALE * S3) * z,
        (SCALE * S15) * (x * y),
        (SCALE * S15) * (y * z),
        (SCALE * 0.5 * S5) * (3.0 * z * z - 1.0),
        (SCALE * S15) * (x * z),
        (SCALE * 0.5 * S15) * (x * x - y * y),
        x,
        y,
        z,
        inv,
        jnp.where(inside, left * left, 0.0),
        jnp.where(inside, (-4.0 / CUTOFF) * scaled * left, 0.0),
    ]
    for number, value in enumerate(values):
        geo_d[number * DENSE : (number + 1) * DENSE, :] = value
    sine, cosine = sin_cos(d * (math.pi / CUTOFF))
    twice = 2.0 * cosine
    sine_last, cosine_last = jnp.zeros_like(sine), jnp.ones_like(sine)
    root = math.sqrt(2.0 / CUTOFF)
    for number in range(8):
        bessel = root * sine * inv
        bes_d[number * DENSE : (number + 1) * DENSE, :] = bessel
        slope_d[number * DENSE : (number + 1) * DENSE, :] = (
            (root * (math.pi / CUTOFF) * (number + 1)) * cosine - bessel
        ) * inv
        sine, sine_last = twice * sine - sine_last, sine
        cosine, cosine_last = twice * cosine - cosine_last, cosine

    def radial_step(step):
        basis = jnp.concatenate([get_eight(bes_d, step), get_eight(slope_d, step)], axis=1)
        a, b, c = split3(basis)
        zero = jnp.zeros_like(a)
        stack = jnp.concatenate([a, b, a, b, c, a, zero, zero], axis=0).astype(BF16)
        both = mm(w6[...], stack)
        u, u_d = both[:, :TILE], both[:, TILE:]
        gate = 1.0 / (1.0 + jnp.exp(-u))
        hidden = u * gate
        slope = gate + hidden * (1.0 - gate)
        env, env_d = get_row(geo_d, 13, step), get_row(geo_d, 14, step)
        g = jnp.concatenate([env * hidden, env_d * hidden + env * (slope * u_d)], axis=1)
        hi, lo = split2(g)
        radial = mm(w3[...], jnp.concatenate([hi, lo, hi], axis=0))
        r_s[:, span(step)] = radial[:, :TILE]
        rp_s[:, span(step)] = radial[:, TILE:]

    loop(0, STEPS, radial_step, UNROLL_RADIAL)

    def messages(target, step, signs, features, degrees):
        radial = r_s[:, span(step)]
        for degree in degrees:
            product = radial[degree * CH : (degree + 1) * CH] * features
            for q in range(9):
                if DEGREE[q] != degree:
                    continue
                shape = get_row(geo_d, q, step)
                hi, lo = split2((shape * product) if signs[q] > 0 else (-shape * product))
                target[q * CH : (q + 1) * CH, 0:TILE] = hi
                target[q * CH : (q + 1) * CH, TILE : 2 * TILE] = lo

    s2a[...] = jnp.zeros_like(s2a)
    s2b[...] = jnp.zeros_like(s2b)

    def other_step(group):
        degrees, start, stop = GROUPS[group]

        def one(step):
            messages(m_s, step, PARITY, fa_s[:, span(step)], degrees)
            table = oh2[OWN:EXT, span(step)]
            table = jnp.concatenate([table, table], axis=1)
            s2[group][...] += mm(table, m_s[start:stop, :], NT)

        return one

    def push_sums_y(group):
        base = 4 + 2 * group
        src, dst = s2[group], rsy[group]
        return (
            push(base, src.at[pl.ds(OWN, GY)], dst.at[pl.ds(GY, GY)], y_low),
            push(base + 1, src.at[pl.ds(OWN + GY, GY)], dst.at[pl.ds(0, GY)], y_high),
        )

    def push_sums_x(group):
        base = 8 + 2 * group
        src, dst = s2[group], rsx[group]
        return (
            push(base, src.at[pl.ds(0, GX)], dst.at[pl.ds(GX, GX)], x_low),
            push(base + 1, src.at[pl.ds(GX, GX)], dst.at[pl.ds(0, GX)], x_high),
        )

    def add_sums_y(group):
        if comm:
            hi, lo = split2(rsy[group][...])
            table = ohy_t[OWN : 2 * OWN, 0 : 2 * GY]
            s2[group][0:OWN, :] += mm(table, hi) + mm(table, lo)

    s1[...] = jnp.zeros_like(s1)

    def own_sum_step(step):
        messages(m_s, step, (1.0,) * 9, fb_s[:, span(step)], (0, 1, 2))
        messages(m2_s, step, PARITY, fa_s[:, span(step)], (0, 1, 2))
        table1, table2 = oh1[:, span(step)], oh2[0:OWN, span(step)]
        s1[...] += mm(m_s[...], jnp.concatenate([table1, table1], axis=1), NT) + mm(
            m2_s[...], jnp.concatenate([table2, table2], axis=1), NT
        )

    other_step_a, other_step_b = other_step(0), other_step(1)
    loop(0, STEPS, other_step_a, UNROLL_SUMS)
    y_a = push_sums_y(0)
    loop(0, STEPS, other_step_b, UNROLL_SUMS)
    y_b = push_sums_y(1)
    loop(0, STEPS // 2, own_sum_step, UNROLL_SUMS)
    settle(*y_a)
    add_sums_y(0)
    x_a = push_sums_x(0)
    loop(STEPS // 2, STEPS, own_sum_step, UNROLL_SUMS)
    settle(*y_b)
    add_sums_y(1)
    x_b = push_sums_x(1)

    def home_sums(group):
        _, start, stop = GROUPS[group]
        total = s1[start:stop, :]
        if comm:
            hi, lo = split2(rsx[group][...])
            total = total + (home_y[group] + mm(ohx_t, hi) + mm(ohx_t, lo)).T
        return total

    home_y = []
    for group in range(2):
        hi, lo = split2(rsy[group][...])
        table = ohy_t[0:OWN, 0 : 2 * GY]
        home_y.append(mm(table, hi) + mm(table, lo))

    settle(*x_a)
    sums_a = home_sums(0)
    settle(*x_b)
    sums_b = home_sums(1)

    sums = jnp.concatenate([sums_b, sums_a], axis=0)
    squares = [sums[q * CH : (q + 1) * CH] * sums[q * CH : (q + 1) * CH] for q in range(9)]
    invariant = jnp.concatenate(
        [
            squares[0],
            squares[1] + squares[2] + squares[3],
            squares[4] + squares[5] + squares[6] + squares[7] + squares[8],
        ],
        axis=0,
    )
    mixed = mm(mix_ref[...], invariant, precision=HIGHEST) + feat_ref[...].astype(F32)
    gate = 1.0 / (1.0 + jnp.exp(-mixed))
    diagonal = iota((CH, CH), 0) == iota((CH, CH), 1)
    weight = jnp.sum(jnp.where(diagonal, outw_ref[...], 0.0), axis=1, keepdims=True)
    energy = jnp.sum(weight * (mixed * gate), axis=0, keepdims=True)
    kind = spec_ref[...]
    shift = jnp.zeros_like(energy)
    for k in range(5):
        shift = jnp.where(kind == k, se_ref[k], shift)
    out_ref[3:4, :] = energy + shift
    d_mixed = weight * (gate * (1.0 + mixed * (1.0 - gate)))
    d_inv = 2.0 * mm(mix_ref[...].T, d_mixed, precision=HIGHEST)
    gext[...] = jnp.zeros_like(gext)
    for q in range(9):
        at = slice(q * CH, (q + 1) * CH)
        gradient = sums[at] * d_inv[DEGREE[q] * CH : (DEGREE[q] + 1) * CH]
        hi, lo = split2(gradient)
        gown[at, 0:OWN] = hi
        gown[at, OWN : 2 * OWN] = lo
        hi, lo = split2(PARITY[q] * gradient)
        gown2[at, 0:OWN] = hi
        gown2[at, OWN : 2 * OWN] = lo

    def own_rows(table, group):
        _, start, stop = GROUPS[group]
        return mm(table, gown2[start:stop, 0:OWN], NT) + mm(
            table, gown2[start:stop, OWN : 2 * OWN], NT
        )

    def push_gradient_x(group):
        base = 12 + 2 * group
        src, dst = sgx[group], rgx[group]
        src[...] = own_rows(ohx, group)
        return (
            push(base, src.at[pl.ds(0, GX)], dst.at[pl.ds(GX, GX)], x_low),
            push(base + 1, src.at[pl.ds(GX, GX)], dst.at[pl.ds(0, GX)], x_high),
        )

    def push_gradient_y(group, outgoing):
        base = 16 + 2 * group
        src, dst = sgy[group], rgy[group]
        if comm:
            hi, lo = split2(rgx[group][...])
            table = ohy[0 : 2 * GY, OWN : 2 * OWN]
            outgoing = outgoing + mm(table, hi) + mm(table, lo)
        src[...] = outgoing
        return (
            push(base, src.at[pl.ds(0, GY)], dst.at[pl.ds(GY, GY)], y_low),
            push(base + 1, src.at[pl.ds(GY, GY)], dst.at[pl.ds(0, GY)], y_high),
        )

    def store_ghosts(group, ref, start):
        if comm:
            _, first, last = GROUPS[group]
            hi, lo = split2(ref[...].T)
            width = ref.shape[0]
            gext[first:last, start : start + width] = hi
            gext[first:last, 2 * OWN + start : 2 * OWN + start + width] = lo

    x_a = push_gradient_x(0)
    x_b = push_gradient_x(1)
    outgoing_a = own_rows(ohy[0 : 2 * GY, 0:OWN], 0)
    outgoing_b = own_rows(ohy[0 : 2 * GY, 0:OWN], 1)

    def contract(step, terms, first_row, target, degrees, last):
        along = None
        for degree in degrees:
            part = slice(degree * CH, (degree + 1) * CH)
            radial, slope = r_s[part, span(step)], rp_s[part, span(step)]
            total = None
            for q in range(9):
                if DEGREE[q] != degree:
                    continue
                rows = slice(q * CH - first_row, (q + 1) * CH - first_row)
                here = None
                for gathered, features in terms:
                    product = gathered[rows] * features
                    here = product if here is None else here + product
                put_row(target, q, step, jnp.sum(radial * here, axis=0, keepdims=True))
                term = get_row(geo_d, q, step) * here
                total = term if total is None else total + term
            along = slope * total if along is None else along + slope * total
        put_row(target, last, step, jnp.sum(along, axis=0, keepdims=True))

    def own_step(step):
        table1, table2 = oh1[:, span(step)], oh2[0:OWN, span(step)]
        first = mm(gown[...], jnp.concatenate([table1, table1], axis=0))
        second = mm(gown2[...], jnp.concatenate([table2, table2], axis=0))
        terms = ((first, fb_s[:, span(step)]), (second, fa_s[:, span(step)]))
        contract(step, terms, 0, z_own, (0, 1, 2), 9)

    loop(0, STEPS, own_step, UNROLL_BACK)
    settle(*x_a)
    y_a = push_gradient_y(0, outgoing_a)
    store_ghosts(0, rgxa, 0)
    settle(*x_b)
    y_b = push_gradient_y(1, outgoing_b)
    store_ghosts(1, rgxb, 0)

    def ext_step(group):
        degrees, first, last = GROUPS[group]

        def one(step):
            table = oh2[OWN:EXT_PAD, span(step)]
            gathered = mm(gext[first:last, :], jnp.concatenate([table, table], axis=0))
            terms = ((gathered, fa_s[:, span(step)]),)
            contract(step, terms, first, z_ext, degrees, 9 + group)

        return one

    ext_step_a, ext_step_b = ext_step(0), ext_step(1)
    settle(*y_a)
    store_ghosts(0, rgya, OWN)
    loop(0, STEPS, ext_step_a, UNROLL_BACK)
    settle(*y_b)
    store_ghosts(1, rgyb, OWN)
    loop(0, STEPS, ext_step_b, UNROLL_BACK)

    zs = [dense(z_own, q) + dense(z_ext, q) for q in range(10)]
    zs[9] = zs[9] + dense(z_ext, 10)
    nx, ny, nz, inv = [dense(geo_d, number) for number in range(9, 13)]
    factor = SCALE * inv
    gx = factor * (S3 * zs[1] + S15 * (ny * zs[4] + nz * zs[7] + nx * zs[8]))
    gy = factor * (S3 * zs[2] + S15 * (nx * zs[4] + nz * zs[5] - ny * zs[8]))
    gz = factor * (S3 * zs[3] + S15 * (ny * zs[5] + nx * zs[7]) + (3.0 * S5) * (nz * zs[6]))
    along = zs[9] - (gx * nx + gy * ny + gz * nz)
    pull_d[...] = jnp.zeros_like(pull_d)
    for number, value in enumerate([gx + along * nx, gy + along * ny, gz + along * nz]):
        pull_d[number * DENSE : (number + 1) * DENSE, :] = value
    for step in range(STEPS):
        pulled = get_eight(pull_d, step)
        hi = pulled.astype(BF16).astype(F32)
        pieces_s[:, step * TILE : (step + 1) * TILE] = jnp.concatenate(
            [hi, pulled - hi], axis=0
        ).astype(BF16)
    at_first = mm(oh1[...], pieces_s[...], NT)
    at_second = mm(oh2[...], pieces_s[...], NT)

    def home(rows8, table):
        a, b, c = split3(rows8)
        out = mm(jnp.concatenate([a, b, c, jnp.zeros_like(a)], axis=0).astype(BF16), table)
        return out[0:8] + out[8:16] + out[16:24]

    at_first, at_second = at_first.T, -at_second.T
    at_first = at_first[0:8] + at_first[8:16]
    total = at_second[0:8] + at_second[8:16]
    send_f[0] = total[:, 2 * OWN : 3 * OWN]
    c0 = push(20, send_f.at[0], recv_f.at[1], y_low)
    c1 = push(21, send_f.at[0], recv_f.at[0], y_high)
    settle(c0, c1)
    near = jnp.concatenate([total[:, 0:OWN] + at_first, total[:, OWN : 2 * OWN]], axis=1)
    if comm:
        near = near + home(fold_y(recv_f[0], recv_f[1]), ohy)
    send_f[1] = near[:, OWN : 2 * OWN]
    c0 = push(22, send_f.at[1], recv_f.at[3], x_low)
    c1 = push(23, send_f.at[1], recv_f.at[2], x_high)
    settle(c0, c1)
    own = near[:, 0:OWN]
    if comm:
        own = own + home(fold_x(recv_f[2], recv_f[3]), ohx)
    out_ref[0:3, :] = own[0:3]


def run(args, n_gx, n_gy, comm=True):
    (
        positions,
        features,
        species,
        edge_list,
        edge_count,
        send_list_x,
        send_list_y,
        radial_in,
        radial_out,
        mix_weight,
        out_weight,
        species_energy,
    ) = args
    vmem = pl.BlockSpec(memory_space=pltpu.VMEM)
    smem = pl.BlockSpec(memory_space=pltpu.SMEM)
    scratch = [
        pltpu.VMEM((8, OWN), F32),
        pltpu.VMEM((1, OWN), jnp.int32),
        pltpu.VMEM((OWN, SLOTS), BF16),
        pltpu.VMEM((EXT_PAD, SLOTS), BF16),
        pltpu.VMEM((2, CH // 2 + 8, OWN), F32),
        pltpu.VMEM((2, CH // 2 + 8, OWN), F32),
        pltpu.VMEM((CH + 8, OWN), F32),
        pltpu.VMEM((2, CH + 8, OWN), F32),
        pltpu.VMEM((CH + 32, EXT_PAD), BF16),
        pltpu.VMEM((8, SLOTS), F32),
        pltpu.VMEM((3 * DENSE, OWN), F32),
        pltpu.VMEM((8 * DENSE, OWN), F32),
        pltpu.VMEM((8 * DENSE, OWN), F32),
        pltpu.VMEM((16 * DENSE, OWN), F32),
        pltpu.VMEM((8 * DENSE, OWN), F32),
        pltpu.VMEM((CH, SLOTS), F32),
        pltpu.VMEM((CH, SLOTS), F32),
        pltpu.VMEM((3 * CH, SLOTS), F32),
        pltpu.VMEM((3 * CH, SLOTS), F32),
        pltpu.VMEM((3 * CH, 3 * CH), BF16),
        pltpu.VMEM((CH, 64), BF16),
        pltpu.VMEM((ROWS, 2 * TILE), BF16),
        pltpu.VMEM((ROWS, 2 * TILE), BF16),
        pltpu.VMEM((ROWS, OWN), F32),
        pltpu.VMEM((EXT - OWN, 5 * CH), F32),
        pltpu.VMEM((EXT - OWN, 4 * CH), F32),
        pltpu.VMEM((2 * GY, 5 * CH), F32),
        pltpu.VMEM((2 * GY, 4 * CH), F32),
        pltpu.VMEM((2 * GX, 5 * CH), F32),
        pltpu.VMEM((2 * GX, 4 * CH), F32),
        pltpu.VMEM((ROWS, 2 * OWN), BF16),
        pltpu.VMEM((ROWS, 2 * OWN), BF16),
        pltpu.VMEM((ROWS, 4 * OWN), BF16),
        pltpu.VMEM((2 * GX, 5 * CH), F32),
        pltpu.VMEM((2 * GX, 4 * CH), F32),
        pltpu.VMEM((2 * GX, 5 * CH), F32),
        pltpu.VMEM((2 * GX, 4 * CH), F32),
        pltpu.VMEM((2 * GY, 5 * CH), F32),
        pltpu.VMEM((2 * GY, 4 * CH), F32),
        pltpu.VMEM((2 * GY, 5 * CH), F32),
        pltpu.VMEM((2 * GY, 4 * CH), F32),
        pltpu.VMEM((10 * DENSE, OWN), F32),
        pltpu.VMEM((11 * DENSE, OWN), F32),
        pltpu.VMEM((16, SLOTS), BF16),
        pltpu.VMEM((2, 8, OWN), F32),
        pltpu.VMEM((4, 8, OWN), F32),
        pltpu.SemaphoreType.DMA((24,)),
        pltpu.SemaphoreType.DMA((24,)),
    ]
    params = {"collective_id": 0, "has_side_effects": True} if comm else {}
    both = pl.pallas_call(
        functools.partial(body, comm, n_gx, n_gy),
        out_shape=jax.ShapeDtypeStruct((4, OWN), F32),
        in_specs=[vmem, vmem, vmem, vmem, smem, vmem, vmem, vmem, vmem, vmem, vmem, smem],
        out_specs=vmem,
        scratch_shapes=scratch,
        compiler_params=pltpu.CompilerParams(vmem_limit_bytes=60 * 1024 * 1024, **params),
        name="layer",
    )(
        positions,
        features,
        species.reshape(1, -1),
        edge_list,
        edge_count,
        send_list_x.reshape(1, -1),
        send_list_y.reshape(1, -1),
        radial_in.T,
        radial_out.T,
        mix_weight,
        out_weight.reshape(1, -1),
        species_energy,
    )
    return both[3], both[0:3]


def solution(mesh):
    n_gx, n_gy = mesh.shape["gx"], mesh.shape["gy"]
    both = ("gx", "gy")
    placed = (
        P(None, both),
        P(None, both),
        P(both),
        P(None, both),
        P(both),
        P(both),
        P(both),
        P(),
        P(),
        P(),
        P(),
        P(),
    )
    return jax.shard_map(
        lambda *args: run(args, n_gx, n_gy),
        mesh=mesh,
        in_specs=placed,
        out_specs=(P(both), P(None, both)),
        check_vma=False,
    )
```

```python
import functools
import math

import jax
import jax.numpy as jnp
from jax import lax
from jax.experimental import pallas as pl
from jax.experimental.pallas import tpu as pltpu
from jax.sharding import PartitionSpec as P

MESH = pl.DeviceIdType.MESH
F32 = jnp.float32
BF16 = jnp.bfloat16
HIGHEST = lax.Precision.HIGHEST

CH = 64
OWN = 128
GX = 64
GY = 32
EXT = 320
EXT_PAD = 384
TILE = 256
STEPS = 13
SLOTS = TILE * STEPS
ROWS = 9 * CH
DENSE = 32

CUTOFF = 5.0
SCALE = 0.3
S3 = math.sqrt(3.0)
S5 = math.sqrt(5.0)
S15 = math.sqrt(15.0)
DEGREE = (0, 1, 1, 1, 2, 2, 2, 2, 2)
GROUPS = (((2,), 256, 576), ((0, 1), 0, 256))
PARITY = (1.0, -1.0, -1.0, -1.0, 1.0, 1.0, 1.0, 1.0, 1.0)

UNROLL_GATHER = True
UNROLL_RADIAL = True
UNROLL_SUMS = True
UNROLL_BACK = True

NN = (((1,), (0,)), ((), ()))
NT = (((1,), (1,)), ((), ()))


def mm(a, b, dims=NN, precision=None):
    return lax.dot_general(a, b, dims, precision=precision, preferred_element_type=F32)


def split2(x):
    hi = x.astype(BF16)
    return hi, (x - hi.astype(F32)).astype(BF16)


def split3(x):
    a = x.astype(BF16).astype(F32)
    b = (x - a).astype(BF16).astype(F32)
    return a, b, (x - a) - b


def iota(shape, dim):
    return lax.broadcasted_iota(jnp.int32, shape, dim)


def onehot(cond):
    return jnp.where(cond, 1.0, 0.0)


def sin_cos(arg):
    k = jnp.floor(arg * (1.0 / math.pi) + 0.5)
    r = (arg - k * 3.140625) - k * (math.pi - 3.140625)
    sign = 1.0 - 2.0 * (k - 2.0 * jnp.floor(k * 0.5))
    r2 = r * r
    s = 1.0 / 6227020800.0
    for c in (-1.0 / 39916800, 1.0 / 362880, -1.0 / 5040, 1.0 / 120, -1.0 / 6, 1.0):
        s = s * r2 + c
    q = -1.0 / 87178291200.0
    for c in (1.0 / 479001600, -1.0 / 3628800, 1.0 / 40320, -1.0 / 720, 1.0 / 24, -0.5, 1.0):
        q = q * r2 + c
    return sign * (s * r), sign * q


def body(
    comm,
    n_gx,
    n_gy,
    pos_ref,
    feat_ref,
    spec_ref,
    edge_ref,
    cnt_ref,
    slx_ref,
    sly_ref,
    win_ref,
    wout_ref,
    mix_ref,
    outw_ref,
    se_ref,
    energy_ref,
    force_ref,
    pos8,
    slyp,
    oh1,
    oh2,
    send_x,
    recv_x,
    send_y,
    recv_y,
    ext_l,
    pa_s,
    rel_d,
    bes_d,
    slope_d,
    geo_d,
    pull_d,
    fa_s,
    fb_s,
    r_s,
    rp_s,
    w3,
    w6,
    m_s,
    s1,
    s2a,
    s2b,
    rsya,
    rsyb,
    rsxa,
    rsxb,
    gown,
    gown2,
    gext,
    sgxa,
    sgxb,
    rgxa,
    rgxb,
    sgya,
    sgyb,
    rgya,
    rgyb,
    z_own,
    z_ext,
    pieces_s,
    send_f,
    recv_f,
    send_sem,
    recv_sem,
):
    s2, rsy, rsx = (s2a, s2b), (rsya, rsyb), (rsxa, rsxb)
    sgx, rgx, sgy, rgy = (sgxa, sgxb), (rgxa, rgxb), (sgya, sgyb), (rgya, rgyb)
    if comm:
        ix = lax.axis_index("gx")
        iy = lax.axis_index("gy")
        x_low = (lax.rem(ix + n_gx - 1, n_gx), iy)
        x_high = (lax.rem(ix + 1, n_gx), iy)
        y_low = (ix, lax.rem(iy + n_gy - 1, n_gy))
        y_high = (ix, lax.rem(iy + 1, n_gy))
        barrier = pltpu.get_barrier_semaphore()
        for device in (x_low, x_high, y_low, y_high):
            pl.semaphore_signal(barrier, inc=1, device_id=device, device_id_type=MESH)
    else:
        x_low = x_high = y_low = y_high = None

    def push(number, src, dst, device):
        if not comm:
            return None
        copy = pltpu.make_async_remote_copy(
            src_ref=src,
            dst_ref=dst,
            send_sem=send_sem.at[number],
            recv_sem=recv_sem.at[number],
            device_id=device,
            device_id_type=MESH,
        )
        copy.start()
        return copy

    def settle(*copies):
        for copy in copies:
            if copy is not None:
                copy.wait()

    lane = iota((1, OWN), 1)

    slyp[...] = jnp.full_like(slyp, -1)
    slyp[:, 0 : 2 * GY] = sly_ref[...]
    ohx_t32 = onehot(iota((OWN, OWN), 0) == slx_ref[...])
    ohy_t32 = onehot(iota((2 * OWN, OWN), 0) == slyp[...])
    ohx_t = ohx_t32.astype(BF16)
    ohy_t = ohy_t32.astype(BF16)
    ohx = ohx_t32.T.astype(BF16)
    ohy = ohy_t32.T.astype(BF16)

    def pack(rows72):
        a, b, c = split3(rows72[CH : CH + 8])
        pieces = jnp.concatenate([a, b, c, jnp.zeros_like(a)], axis=0).astype(BF16)
        return jnp.concatenate([rows72[:CH].astype(BF16), pieces], axis=0)

    def unpack(rows96):
        return (rows96[CH : CH + 8] + rows96[CH + 8 : CH + 16]) + rows96[CH + 16 : CH + 24]

    def fold_x(low, high):
        return jnp.where(lane < GX, pltpu.roll(low, GX, 1), pltpu.roll(high, GX, 1))

    def fold_y(low, high):
        picked = jnp.where(lane < GY, pltpu.roll(low, OWN - GY, 1), pltpu.roll(high, GY, 1))
        return jnp.where(lane < 2 * GY, picked, 0.0)

    pos8[...] = jnp.zeros_like(pos8)
    pos8[0:3, :] = pos_ref[...]
    own_l = pack(jnp.concatenate([feat_ref[...].astype(F32), pos8[...]], axis=0))
    ext_l[:, 0:OWN] = own_l
    picked = mm(own_l, ohx_t)
    half = CH // 2
    upper, lower = picked[0:half], picked[half:CH]
    near_low = lane < GX
    send_x[0, 0:half, :] = jnp.where(near_low, upper, pltpu.roll(lower, GX, 1))
    send_x[1, 0:half, :] = jnp.where(near_low, pltpu.roll(upper, GX, 1), lower)
    coordinates = unpack(picked)
    send_x[0, half:, :] = coordinates
    send_x[1, half:, :] = coordinates
    if comm:
        pl.semaphore_wait(barrier, 4)
    c0 = push(0, send_x.at[0], recv_x.at[1], x_low)
    c1 = push(1, send_x.at[1], recv_x.at[0], x_high)

    hi, lo = split2(wout_ref[...])
    hi, lo = hi.astype(F32), lo.astype(F32)
    w3[...] = jnp.concatenate([hi, hi, lo], axis=0).T.astype(BF16)
    a, b, c = split3(win_ref[...])
    zero = jnp.zeros_like(a)
    w6[...] = jnp.concatenate([a, a, b, b, a, c, zero, zero], axis=0).T.astype(BF16)
    count = cnt_ref[0]

    def table_step(step, carry):
        at = pl.ds(pl.multiple_of(step * TILE, TILE), TILE)
        live = iota((1, TILE), 1) + step * TILE < count
        first = jnp.where(live, edge_ref[0:1, at], -1)
        second = jnp.where(live, edge_ref[1:2, at], -1)
        table1 = onehot(iota((OWN, TILE), 0) == first).astype(BF16)
        oh1[:, at] = table1
        oh2[:, at] = onehot(iota((EXT_PAD, TILE), 0) == second).astype(BF16)
        got = mm(ext_l[:, 0:OWN], table1)
        fa_s[:, at] = got[0:CH]
        pa_s[:, at] = unpack(got)
        return carry

    lax.fori_loop(0, STEPS, table_step, 0)

    settle(c0, c1)
    if comm:
        low, high = recv_x[0], recv_x[1]
        turned_low, turned_high = pltpu.roll(low, GX, 1), pltpu.roll(high, GX, 1)
        upper = jnp.where(near_low, low[0:half], turned_high[0:half])
        lower = jnp.where(near_low, turned_low[0:half], high[0:half])
        coordinates = jnp.where(near_low, turned_low[half:], turned_high[half:])
        section = pack(jnp.concatenate([upper, lower, coordinates], axis=0))
    else:
        section = own_l
    ext_l[:, OWN : 2 * OWN] = section
    picked = mm(own_l, ohy_t[0:OWN]) + mm(section, ohy_t[OWN : 2 * OWN])
    send_y[0:CH, :] = picked[0:CH]
    send_y[CH : CH + 8, :] = unpack(picked)
    c0 = push(2, send_y, recv_y.at[1], y_low)
    c1 = push(3, send_y, recv_y.at[0], y_high)
    settle(c0, c1)
    if comm:
        ext_l[:, 2 * OWN : 3 * OWN] = pack(fold_y(recv_y[0], recv_y[1]))
    else:
        ext_l[:, 2 * OWN : 3 * OWN] = jnp.where(lane < 2 * GY, own_l, 0.0)

    def span(step):
        return pl.ds(pl.multiple_of(step * TILE, TILE), TILE)

    def loop(start, stop, step_fn, unroll):
        def one(step, carry):
            step_fn(step)
            return carry

        lax.fori_loop(start, stop, one, 0, unroll=unroll)

    def ahead(start, stop, fetch, use, unroll):
        def one(step, value):
            following = fetch(jnp.minimum(step + 1, stop - 1))
            use(step, value)
            return following

        lax.fori_loop(start, stop, one, fetch(start), unroll=unroll)

    def halves(value):
        return value[:, 0:OWN], value[:, OWN:TILE]

    def get_row(ref, number, step):
        at = number * DENSE + 2 * step
        return jnp.concatenate([ref[pl.ds(at, 1), :], ref[pl.ds(at + 1, 1), :]], axis=1)

    def put_row(ref, number, step, value):
        at = number * DENSE + 2 * step
        low, high = halves(value)
        ref[pl.ds(at, 1), :] = low
        ref[pl.ds(at + 1, 1), :] = high

    def get_eight(ref, step):
        at = 2 * step
        return jnp.concatenate(
            [ref[pl.ds(at, 8, stride=DENSE), :], ref[pl.ds(at + 1, 8, stride=DENSE), :]], axis=1
        )

    def dense(ref, number):
        return ref[number * DENSE : (number + 1) * DENSE, :]

    rel_d[...] = jnp.full_like(rel_d, 2.0)

    def gather_step(step):
        got = mm(ext_l[...], oh2[:, span(step)])
        fb_s[:, span(step)] = got[0:CH]
        relative = unpack(got) - pa_s[:, span(step)]
        for number in range(3):
            put_row(rel_d, number, step, relative[number : number + 1])

    loop(0, STEPS, gather_step, UNROLL_GATHER)

    live = iota((DENSE, OWN), 0) * OWN + iota((DENSE, OWN), 1) < count
    rx = jnp.where(live, dense(rel_d, 0), 2.0)
    ry = jnp.where(live, dense(rel_d, 1), 0.0)
    rz = jnp.where(live, dense(rel_d, 2), 0.0)
    d = jnp.sqrt(rx * rx + ry * ry + rz * rz)
    inv = 1.0 / d
    x, y, z = rx * inv, ry * inv, rz * inv
    scaled = d * (1.0 / CUTOFF)
    left = 1.0 - scaled * scaled
    inside = d < CUTOFF
    values = [
        jnp.full_like(x, SCALE),
        (SCALE * S3) * x,
        (SCALE * S3) * y,
        (SCALE * S3) * z,
        (SCALE * S15) * (x * y),
        (SCALE * S15) * (y * z),
        (SCALE * 0.5 * S5) * (3.0 * z * z - 1.0),
        (SCALE * S15) * (x * z),
        (SCALE * 0.5 * S15) * (x * x - y * y),
        x,
        y,
        z,
        inv,
        jnp.where(inside, left * left, 0.0),
        jnp.where(inside, (-4.0 / CUTOFF) * scaled * left, 0.0),
    ]
    for number, value in enumerate(values):
        geo_d[number * DENSE : (number + 1) * DENSE, :] = value
    sine, cosine = sin_cos(d * (math.pi / CUTOFF))
    twice = 2.0 * cosine
    sine_last, cosine_last = jnp.zeros_like(sine), jnp.ones_like(sine)
    root = math.sqrt(2.0 / CUTOFF)
    for number in range(8):
        bessel = root * sine * inv
        bes_d[number * DENSE : (number + 1) * DENSE, :] = bessel
        slope_d[number * DENSE : (number + 1) * DENSE, :] = (
            (root * (math.pi / CUTOFF) * (number + 1)) * cosine - bessel
        ) * inv
        sine, sine_last = twice * sine - sine_last, sine
        cosine, cosine_last = twice * cosine - cosine_last, cosine

    def radial_fetch(step):
        basis = jnp.concatenate([get_eight(bes_d, step), get_eight(slope_d, step)], axis=1)
        a, b, c = split3(basis)
        zero = jnp.zeros_like(a)
        stack = jnp.concatenate([a, b, a, b, c, a, zero, zero], axis=0).astype(BF16)
        return mm(w6[...], stack)

    def radial_use(step, both):
        u, u_d = both[:, :TILE], both[:, TILE:]
        gate = 1.0 / (1.0 + jnp.exp(-u))
        hidden = u * gate
        slope = gate + hidden * (1.0 - gate)
        env, env_d = get_row(geo_d, 13, step), get_row(geo_d, 14, step)
        g = jnp.concatenate([env * hidden, env_d * hidden + env * (slope * u_d)], axis=1)
        hi, lo = split2(g)
        radial = mm(w3[...], jnp.concatenate([hi, lo, hi], axis=0))
        r_s[:, span(step)] = radial[:, :TILE]
        rp_s[:, span(step)] = radial[:, TILE:]

    ahead(0, STEPS, radial_fetch, radial_use, UNROLL_RADIAL)

    def messages(target, step, signs, features, degrees):
        radial = r_s[:, span(step)]
        for degree in degrees:
            product = radial[degree * CH : (degree + 1) * CH] * features
            for q in range(9):
                if DEGREE[q] != degree:
                    continue
                shape = get_row(geo_d, q, step)
                hi, lo = split2((shape * product) if signs[q] > 0 else (-shape * product))
                target[q * CH : (q + 1) * CH, 0:TILE] = hi
                target[q * CH : (q + 1) * CH, TILE : 2 * TILE] = lo

    s2a[...] = jnp.zeros_like(s2a)
    s2b[...] = jnp.zeros_like(s2b)

    def other_step(group):
        degrees, start, stop = GROUPS[group]

        def one(step):
            buffer = m_s.at[lax.rem(step, 2)]
            messages(buffer, step, PARITY, fa_s[:, span(step)], degrees)
            table = oh2[OWN:EXT, span(step)]
            table = jnp.concatenate([table, table], axis=1)
            s2[group][...] += mm(table, buffer[start:stop, :], NT)

        return one

    def push_sums_y(group):
        base = 4 + 2 * group
        src, dst = s2[group], rsy[group]
        return (
            push(base, src.at[pl.ds(OWN, GY)], dst.at[pl.ds(GY, GY)], y_low),
            push(base + 1, src.at[pl.ds(OWN + GY, GY)], dst.at[pl.ds(0, GY)], y_high),
        )

    def push_sums_x(group):
        base = 8 + 2 * group
        src, dst = s2[group], rsx[group]
        return (
            push(base, src.at[pl.ds(0, GX)], dst.at[pl.ds(GX, GX)], x_low),
            push(base + 1, src.at[pl.ds(GX, GX)], dst.at[pl.ds(0, GX)], x_high),
        )

    def add_sums_y(group):
        if comm:
            hi, lo = split2(rsy[group][...])
            table = ohy_t[OWN : 2 * OWN, 0 : 2 * GY]
            s2[group][0:OWN, :] += mm(table, hi) + mm(table, lo)

    s1[...] = jnp.zeros_like(s1)

    def own_sum_step(step):
        messages(m_s.at[0], step, (1.0,) * 9, fb_s[:, span(step)], (0, 1, 2))
        messages(m_s.at[1], step, PARITY, fa_s[:, span(step)], (0, 1, 2))
        table1, table2 = oh1[:, span(step)], oh2[0:OWN, span(step)]
        s1[...] += mm(m_s[0], jnp.concatenate([table1, table1], axis=1), NT) + mm(
            m_s[1], jnp.concatenate([table2, table2], axis=1), NT
        )

    other_step_a, other_step_b = other_step(0), other_step(1)
    loop(0, STEPS, other_step_a, UNROLL_SUMS)
    y_a = push_sums_y(0)
    loop(0, STEPS, other_step_b, UNROLL_SUMS)
    y_b = push_sums_y(1)
    loop(0, STEPS // 2, own_sum_step, UNROLL_SUMS)
    settle(*y_a)
    add_sums_y(0)
    x_a = push_sums_x(0)
    loop(STEPS // 2, STEPS, own_sum_step, UNROLL_SUMS)
    settle(*y_b)
    add_sums_y(1)
    x_b = push_sums_x(1)

    def home_sums(group):
        _, start, stop = GROUPS[group]
        total = s1[start:stop, :]
        if comm:
            hi, lo = split2(rsx[group][...])
            total = total + (home_y[group] + mm(ohx_t, hi) + mm(ohx_t, lo)).T
        return total

    home_y = []
    for group in range(2):
        hi, lo = split2(rsy[group][...])
        table = ohy_t[0:OWN, 0 : 2 * GY]
        home_y.append(mm(table, hi) + mm(table, lo))

    settle(*x_a)
    sums_a = home_sums(0)
    settle(*x_b)
    sums_b = home_sums(1)

    sums = jnp.concatenate([sums_b, sums_a], axis=0)
    squares = [sums[q * CH : (q + 1) * CH] * sums[q * CH : (q + 1) * CH] for q in range(9)]
    invariant = jnp.concatenate(
        [
            squares[0],
            squares[1] + squares[2] + squares[3],
            squares[4] + squares[5] + squares[6] + squares[7] + squares[8],
        ],
        axis=0,
    )
    mixed = mm(mix_ref[...], invariant, precision=HIGHEST) + feat_ref[...].astype(F32)
    gate = 1.0 / (1.0 + jnp.exp(-mixed))
    diagonal = iota((CH, CH), 0) == iota((CH, CH), 1)
    weight = jnp.sum(jnp.where(diagonal, outw_ref[...], 0.0), axis=1, keepdims=True)
    energy = jnp.sum(weight * (mixed * gate), axis=0, keepdims=True)
    kind = spec_ref[...]
    shift = jnp.zeros_like(energy)
    for k in range(5):
        shift = jnp.where(kind == k, se_ref[k], shift)
    energy_ref[...] = energy + shift
    d_mixed = weight * (gate * (1.0 + mixed * (1.0 - gate)))
    d_inv = 2.0 * mm(mix_ref[...].T, d_mixed, precision=HIGHEST)
    gext[...] = jnp.zeros_like(gext)
    for q in range(9):
        at = slice(q * CH, (q + 1) * CH)
        gradient = sums[at] * d_inv[DEGREE[q] * CH : (DEGREE[q] + 1) * CH]
        hi, lo = split2(gradient)
        gown[at, 0:OWN] = hi
        gown[at, OWN : 2 * OWN] = lo
        hi, lo = split2(PARITY[q] * gradient)
        gown2[at, 0:OWN] = hi
        gown2[at, OWN : 2 * OWN] = lo

    def own_rows(table, group):
        _, start, stop = GROUPS[group]
        return mm(table, gown2[start:stop, 0:OWN], NT) + mm(
            table, gown2[start:stop, OWN : 2 * OWN], NT
        )

    def push_gradient_x(group):
        base = 12 + 2 * group
        src, dst = sgx[group], rgx[group]
        src[...] = own_rows(ohx, group)
        return (
            push(base, src.at[pl.ds(0, GX)], dst.at[pl.ds(GX, GX)], x_low),
            push(base + 1, src.at[pl.ds(GX, GX)], dst.at[pl.ds(0, GX)], x_high),
        )

    def push_gradient_y(group, outgoing):
        base = 16 + 2 * group
        src, dst = sgy[group], rgy[group]
        if comm:
            hi, lo = split2(rgx[group][...])
            table = ohy[0 : 2 * GY, OWN : 2 * OWN]
            outgoing = outgoing + mm(table, hi) + mm(table, lo)
        src[...] = outgoing
        return (
            push(base, src.at[pl.ds(0, GY)], dst.at[pl.ds(GY, GY)], y_low),
            push(base + 1, src.at[pl.ds(GY, GY)], dst.at[pl.ds(0, GY)], y_high),
        )

    def store_ghosts(group, ref, start):
        if comm:
            _, first, last = GROUPS[group]
            hi, lo = split2(ref[...].T)
            width = ref.shape[0]
            gext[first:last, start : start + width] = hi
            gext[first:last, 2 * OWN + start : 2 * OWN + start + width] = lo

    x_a = push_gradient_x(0)
    x_b = push_gradient_x(1)
    outgoing_a = own_rows(ohy[0 : 2 * GY, 0:OWN], 0)
    outgoing_b = own_rows(ohy[0 : 2 * GY, 0:OWN], 1)

    def contract(step, terms, first_row, target, degrees, last):
        along = None
        for degree in degrees:
            part = slice(degree * CH, (degree + 1) * CH)
            radial, slope = r_s[part, span(step)], rp_s[part, span(step)]
            total = None
            for q in range(9):
                if DEGREE[q] != degree:
                    continue
                rows = slice(q * CH - first_row, (q + 1) * CH - first_row)
                here = None
                for gathered, features in terms:
                    product = gathered[rows] * features
                    here = product if here is None else here + product
                put_row(target, q, step, jnp.sum(radial * here, axis=0, keepdims=True))
                term = get_row(geo_d, q, step) * here
                total = term if total is None else total + term
            along = slope * total if along is None else along + slope * total
        put_row(target, last, step, jnp.sum(along, axis=0, keepdims=True))

    def own_step(step):
        table1, table2 = oh1[:, span(step)], oh2[0:OWN, span(step)]
        first = mm(gown[...], jnp.concatenate([table1, table1], axis=0))
        second = mm(gown2[...], jnp.concatenate([table2, table2], axis=0))
        terms = ((first, fb_s[:, span(step)]), (second, fa_s[:, span(step)]))
        contract(step, terms, 0, z_own, (0, 1, 2), 9)

    loop(0, STEPS, own_step, UNROLL_BACK)
    settle(*x_a)
    y_a = push_gradient_y(0, outgoing_a)
    store_ghosts(0, rgxa, 0)
    settle(*x_b)
    y_b = push_gradient_y(1, outgoing_b)
    store_ghosts(1, rgxb, 0)

    def ext_step(group):
        degrees, first, last = GROUPS[group]

        def fetch(step):
            table = oh2[OWN:EXT_PAD, span(step)]
            return mm(gext[first:last, :], jnp.concatenate([table, table], axis=0))

        def use(step, gathered):
            terms = ((gathered, fa_s[:, span(step)]),)
            contract(step, terms, first, z_ext, degrees, 9 + group)

        return fetch, use

    ext_a, ext_b = ext_step(0), ext_step(1)
    settle(*y_a)
    store_ghosts(0, rgya, OWN)
    ahead(0, STEPS, *ext_a, UNROLL_BACK)
    settle(*y_b)
    store_ghosts(1, rgyb, OWN)
    ahead(0, STEPS, *ext_b, UNROLL_BACK)

    zs = [dense(z_own, q) + dense(z_ext, q) for q in range(10)]
    zs[9] = zs[9] + dense(z_ext, 10)
    nx, ny, nz, inv = [dense(geo_d, number) for number in range(9, 13)]
    factor = SCALE * inv
    gx = factor * (S3 * zs[1] + S15 * (ny * zs[4] + nz * zs[7] + nx * zs[8]))
    gy = factor * (S3 * zs[2] + S15 * (nx * zs[4] + nz * zs[5] - ny * zs[8]))
    gz = factor * (S3 * zs[3] + S15 * (ny * zs[5] + nx * zs[7]) + (3.0 * S5) * (nz * zs[6]))
    along = zs[9] - (gx * nx + gy * ny + gz * nz)
    pull_d[...] = jnp.zeros_like(pull_d)
    for number, value in enumerate([gx + along * nx, gy + along * ny, gz + along * nz]):
        pull_d[number * DENSE : (number + 1) * DENSE, :] = value
    for step in range(STEPS):
        pulled = get_eight(pull_d, step)
        hi = pulled.astype(BF16).astype(F32)
        pieces_s[:, step * TILE : (step + 1) * TILE] = jnp.concatenate(
            [hi, pulled - hi], axis=0
        ).astype(BF16)
    at_first = mm(oh1[...], pieces_s[...], NT)
    at_second = mm(oh2[...], pieces_s[...], NT)

    def home(rows8, table):
        a, b, c = split3(rows8)
        out = mm(jnp.concatenate([a, b, c, jnp.zeros_like(a)], axis=0).astype(BF16), table)
        return out[0:8] + out[8:16] + out[16:24]

    at_first, at_second = at_first.T, -at_second.T
    at_first = at_first[0:8] + at_first[8:16]
    total = at_second[0:8] + at_second[8:16]
    send_f[0] = total[:, 2 * OWN : 3 * OWN]
    c0 = push(20, send_f.at[0], recv_f.at[1], y_low)
    c1 = push(21, send_f.at[0], recv_f.at[0], y_high)
    settle(c0, c1)
    near = jnp.concatenate([total[:, 0:OWN] + at_first, total[:, OWN : 2 * OWN]], axis=1)
    if comm:
        near = near + home(fold_y(recv_f[0], recv_f[1]), ohy)
    send_f[1] = near[:, OWN : 2 * OWN]
    c0 = push(22, send_f.at[1], recv_f.at[3], x_low)
    c1 = push(23, send_f.at[1], recv_f.at[2], x_high)
    settle(c0, c1)
    own = near[:, 0:OWN]
    if comm:
        own = own + home(fold_x(recv_f[2], recv_f[3]), ohx)
    force_ref[...] = own[0:3]


def run(args, n_gx, n_gy, comm=True):
    (
        positions,
        features,
        species,
        edge_list,
        edge_count,
        send_list_x,
        send_list_y,
        radial_in,
        radial_out,
        mix_weight,
        out_weight,
        species_energy,
    ) = args
    vmem = pl.BlockSpec(memory_space=pltpu.VMEM)
    smem = pl.BlockSpec(memory_space=pltpu.SMEM)
    scratch = [
        pltpu.VMEM((8, OWN), F32),
        pltpu.VMEM((1, OWN), jnp.int32),
        pltpu.VMEM((OWN, SLOTS), BF16),
        pltpu.VMEM((EXT_PAD, SLOTS), BF16),
        pltpu.VMEM((2, CH // 2 + 8, OWN), F32),
        pltpu.VMEM((2, CH // 2 + 8, OWN), F32),
        pltpu.VMEM((CH + 8, OWN), F32),
        pltpu.VMEM((2, CH + 8, OWN), F32),
        pltpu.VMEM((CH + 32, EXT_PAD), BF16),
        pltpu.VMEM((8, SLOTS), F32),
        pltpu.VMEM((3 * DENSE, OWN), F32),
        pltpu.VMEM((8 * DENSE, OWN), F32),
        pltpu.VMEM((8 * DENSE, OWN), F32),
        pltpu.VMEM((16 * DENSE, OWN), F32),
        pltpu.VMEM((8 * DENSE, OWN), F32),
        pltpu.VMEM((CH, SLOTS), F32),
        pltpu.VMEM((CH, SLOTS), F32),
        pltpu.VMEM((3 * CH, SLOTS), F32),
        pltpu.VMEM((3 * CH, SLOTS), F32),
        pltpu.VMEM((3 * CH, 3 * CH), BF16),
        pltpu.VMEM((CH, 64), BF16),
        pltpu.VMEM((2, ROWS, 2 * TILE), BF16),
        pltpu.VMEM((ROWS, OWN), F32),
        pltpu.VMEM((EXT - OWN, 5 * CH), F32),
        pltpu.VMEM((EXT - OWN, 4 * CH), F32),
        pltpu.VMEM((2 * GY, 5 * CH), F32),
        pltpu.VMEM((2 * GY, 4 * CH), F32),
        pltpu.VMEM((2 * GX, 5 * CH), F32),
        pltpu.VMEM((2 * GX, 4 * CH), F32),
        pltpu.VMEM((ROWS, 2 * OWN), BF16),
        pltpu.VMEM((ROWS, 2 * OWN), BF16),
        pltpu.VMEM((ROWS, 4 * OWN), BF16),
        pltpu.VMEM((2 * GX, 5 * CH), F32),
        pltpu.VMEM((2 * GX, 4 * CH), F32),
        pltpu.VMEM((2 * GX, 5 * CH), F32),
        pltpu.VMEM((2 * GX, 4 * CH), F32),
        pltpu.VMEM((2 * GY, 5 * CH), F32),
        pltpu.VMEM((2 * GY, 4 * CH), F32),
        pltpu.VMEM((2 * GY, 5 * CH), F32),
        pltpu.VMEM((2 * GY, 4 * CH), F32),
        pltpu.VMEM((10 * DENSE, OWN), F32),
        pltpu.VMEM((11 * DENSE, OWN), F32),
        pltpu.VMEM((16, SLOTS), BF16),
        pltpu.VMEM((2, 8, OWN), F32),
        pltpu.VMEM((4, 8, OWN), F32),
        pltpu.SemaphoreType.DMA((24,)),
        pltpu.SemaphoreType.DMA((24,)),
    ]
    params = {"collective_id": 0, "has_side_effects": True} if comm else {}
    energies, forces = pl.pallas_call(
        functools.partial(body, comm, n_gx, n_gy),
        out_shape=(
            jax.ShapeDtypeStruct((1, OWN), F32),
            jax.ShapeDtypeStruct((3, OWN), F32),
        ),
        in_specs=[vmem, vmem, vmem, vmem, smem, vmem, vmem, vmem, vmem, vmem, vmem, smem],
        out_specs=(vmem, vmem),
        scratch_shapes=scratch,
        compiler_params=pltpu.CompilerParams(vmem_limit_bytes=60 * 1024 * 1024, **params),
        name="layer",
    )(
        positions,
        features,
        species.reshape(1, -1),
        edge_list,
        edge_count,
        send_list_x.reshape(1, -1),
        send_list_y.reshape(1, -1),
        radial_in.T,
        radial_out.T,
        mix_weight,
        out_weight.reshape(1, -1),
        species_energy,
    )
    return energies.reshape(-1), forces


def solution(mesh):
    n_gx, n_gy = mesh.shape["gx"], mesh.shape["gy"]
    both = ("gx", "gy")
    placed = (
        P(None, both),
        P(None, both),
        P(both),
        P(None, both),
        P(both),
        P(both),
        P(both),
        P(),
        P(),
        P(),
        P(),
        P(),
    )
    return jax.shard_map(
        lambda *args: run(args, n_gx, n_gy),
        mesh=mesh,
        in_specs=placed,
        out_specs=(P(both), P(None, both)),
        check_vma=False,
    )
```

```python
import functools
import math

import jax
import jax.numpy as jnp
from jax import lax
from jax.experimental import pallas as pl
from jax.experimental.pallas import tpu as pltpu
from jax.sharding import PartitionSpec as P

MESH = pl.DeviceIdType.MESH
F32 = jnp.float32
BF16 = jnp.bfloat16
HIGHEST = lax.Precision.HIGHEST

CH = 64
OWN = 128
GX = 64
GY = 32
EXT = 320
EXT_PAD = 384
TILE = 256
STEPS = 13
SLOTS = TILE * STEPS
ROWS = 9 * CH
DENSE = 32

CUTOFF = 5.0
SCALE = 0.3
S3 = math.sqrt(3.0)
S5 = math.sqrt(5.0)
S15 = math.sqrt(15.0)
DEGREE = (0, 1, 1, 1, 2, 2, 2, 2, 2)
GROUPS = (((2,), 256, 576), ((0, 1), 0, 256))
PARITY = (1.0, -1.0, -1.0, -1.0, 1.0, 1.0, 1.0, 1.0, 1.0)

UNROLL_GATHER = True
UNROLL_RADIAL = True
UNROLL_SUMS = True
UNROLL_BACK = True

NN = (((1,), (0,)), ((), ()))
NT = (((1,), (1,)), ((), ()))


def mm(a, b, dims=NN, precision=None):
    return lax.dot_general(a, b, dims, precision=precision, preferred_element_type=F32)


def split2(x):
    hi = x.astype(BF16)
    return hi, (x - hi.astype(F32)).astype(BF16)


def split3(x):
    a = x.astype(BF16).astype(F32)
    b = (x - a).astype(BF16).astype(F32)
    return a, b, (x - a) - b


def iota(shape, dim):
    return lax.broadcasted_iota(jnp.int32, shape, dim)


def onehot(cond):
    return jnp.where(cond, 1.0, 0.0)


def sin_cos(arg):
    k = jnp.floor(arg * (1.0 / math.pi) + 0.5)
    r = (arg - k * 3.140625) - k * (math.pi - 3.140625)
    sign = 1.0 - 2.0 * (k - 2.0 * jnp.floor(k * 0.5))
    r2 = r * r
    s = 1.0 / 6227020800.0
    for c in (-1.0 / 39916800, 1.0 / 362880, -1.0 / 5040, 1.0 / 120, -1.0 / 6, 1.0):
        s = s * r2 + c
    q = -1.0 / 87178291200.0
    for c in (1.0 / 479001600, -1.0 / 3628800, 1.0 / 40320, -1.0 / 720, 1.0 / 24, -0.5, 1.0):
        q = q * r2 + c
    return sign * (s * r), sign * q


def body(
    comm,
    n_gx,
    n_gy,
    pos_ref,
    feat_ref,
    spec_ref,
    edge_ref,
    cnt_ref,
    slx_ref,
    sly_ref,
    win_ref,
    wout_ref,
    mix_ref,
    outw_ref,
    se_ref,
    energy_ref,
    force_ref,
    pos8,
    slyp,
    oh1,
    oh2,
    send_x,
    recv_x,
    send_y,
    recv_y,
    ext_l,
    pa_s,
    rel_d,
    bes_d,
    slope_d,
    geo_d,
    pull_d,
    fa_s,
    fb_s,
    r_s,
    rp_s,
    w3,
    w6,
    m_s,
    s1,
    s2a,
    s2b,
    rsya,
    rsyb,
    rsxa,
    rsxb,
    gown,
    gown2,
    gext,
    sgxa,
    sgxb,
    rgxa,
    rgxb,
    sgya,
    sgyb,
    rgya,
    rgyb,
    z_own,
    z_ext,
    pieces_s,
    send_f,
    recv_f,
    send_sem,
    recv_sem,
):
    s2, rsy, rsx = (s2a, s2b), (rsya, rsyb), (rsxa, rsxb)
    sgx, rgx, sgy, rgy = (sgxa, sgxb), (rgxa, rgxb), (sgya, sgyb), (rgya, rgyb)
    if comm:
        ix = lax.axis_index("gx")
        iy = lax.axis_index("gy")
        x_low = (lax.rem(ix + n_gx - 1, n_gx), iy)
        x_high = (lax.rem(ix + 1, n_gx), iy)
        y_low = (ix, lax.rem(iy + n_gy - 1, n_gy))
        y_high = (ix, lax.rem(iy + 1, n_gy))
        barrier = pltpu.get_barrier_semaphore()
        for device in (x_low, x_high, y_low, y_high):
            pl.semaphore_signal(barrier, inc=1, device_id=device, device_id_type=MESH)
    else:
        x_low = x_high = y_low = y_high = None

    def push(number, src, dst, device):
        if not comm:
            return None
        copy = pltpu.make_async_remote_copy(
            src_ref=src,
            dst_ref=dst,
            send_sem=send_sem.at[number],
            recv_sem=recv_sem.at[number],
            device_id=device,
            device_id_type=MESH,
        )
        copy.start()
        return copy

    def settle(*copies):
        for copy in copies:
            if copy is not None:
                copy.wait()

    lane = iota((1, OWN), 1)

    slyp[...] = jnp.full_like(slyp, -1)
    slyp[:, 0 : 2 * GY] = sly_ref[...]
    ohx_t32 = onehot(iota((OWN, OWN), 0) == slx_ref[...])
    ohy_t32 = onehot(iota((2 * OWN, OWN), 0) == slyp[...])
    ohx_t = ohx_t32.astype(BF16)
    ohy_t = ohy_t32.astype(BF16)
    ohx = ohx_t32.T.astype(BF16)
    ohy = ohy_t32.T.astype(BF16)

    def pack(rows72):
        a, b, c = split3(rows72[CH : CH + 8])
        pieces = jnp.concatenate([a, b, c, jnp.zeros_like(a)], axis=0).astype(BF16)
        return jnp.concatenate([rows72[:CH].astype(BF16), pieces], axis=0)

    def unpack(rows96):
        return (rows96[CH : CH + 8] + rows96[CH + 8 : CH + 16]) + rows96[CH + 16 : CH + 24]

    def fold_x(low, high):
        return jnp.where(lane < GX, pltpu.roll(low, GX, 1), pltpu.roll(high, GX, 1))

    def fold_y(low, high):
        picked = jnp.where(lane < GY, pltpu.roll(low, OWN - GY, 1), pltpu.roll(high, GY, 1))
        return jnp.where(lane < 2 * GY, picked, 0.0)

    pos8[...] = jnp.zeros_like(pos8)
    pos8[0:3, :] = pos_ref[...]
    own_l = pack(jnp.concatenate([feat_ref[...].astype(F32), pos8[...]], axis=0))
    ext_l[:, 0:OWN] = own_l
    picked = mm(own_l, ohx_t)
    half = CH // 2
    upper, lower = picked[0:half], picked[half:CH]
    near_low = lane < GX
    send_x[0, 0:half, :] = jnp.where(near_low, upper, pltpu.roll(lower, GX, 1))
    send_x[1, 0:half, :] = jnp.where(near_low, pltpu.roll(upper, GX, 1), lower)
    coordinates = unpack(picked)
    send_x[0, half:, :] = coordinates
    send_x[1, half:, :] = coordinates
    if comm:
        pl.semaphore_wait(barrier, 4)
    c0 = push(0, send_x.at[0], recv_x.at[1], x_low)
    c1 = push(1, send_x.at[1], recv_x.at[0], x_high)

    hi, lo = split2(wout_ref[...])
    hi, lo = hi.astype(F32), lo.astype(F32)
    w3[...] = jnp.concatenate([hi, hi, lo], axis=0).T.astype(BF16)
    a, b, c = split3(win_ref[...])
    zero = jnp.zeros_like(a)
    w6[...] = jnp.concatenate([a, a, b, b, a, c, zero, zero], axis=0).T.astype(BF16)
    count = cnt_ref[0]

    def table_step(step, carry):
        at = pl.ds(pl.multiple_of(step * TILE, TILE), TILE)
        live = iota((1, TILE), 1) + step * TILE < count
        first = jnp.where(live, edge_ref[0:1, at], -1)
        second = jnp.where(live, edge_ref[1:2, at], -1)
        table1 = onehot(iota((OWN, TILE), 0) == first).astype(BF16)
        oh1[:, at] = table1
        oh2[:, at] = onehot(iota((EXT_PAD, TILE), 0) == second).astype(BF16)
        got = mm(ext_l[:, 0:OWN], table1)
        fa_s[:, at] = got[0:CH]
        pa_s[:, at] = unpack(got)
        return carry

    lax.fori_loop(0, STEPS, table_step, 0)

    settle(c0, c1)
    if comm:
        low, high = recv_x[0], recv_x[1]
        turned_low, turned_high = pltpu.roll(low, GX, 1), pltpu.roll(high, GX, 1)
        upper = jnp.where(near_low, low[0:half], turned_high[0:half])
        lower = jnp.where(near_low, turned_low[0:half], high[0:half])
        coordinates = jnp.where(near_low, turned_low[half:], turned_high[half:])
        section = pack(jnp.concatenate([upper, lower, coordinates], axis=0))
    else:
        section = own_l
    ext_l[:, OWN : 2 * OWN] = section
    picked = mm(own_l, ohy_t[0:OWN]) + mm(section, ohy_t[OWN : 2 * OWN])
    send_y[0:CH, :] = picked[0:CH]
    send_y[CH : CH + 8, :] = unpack(picked)
    c0 = push(2, send_y, recv_y.at[1], y_low)
    c1 = push(3, send_y, recv_y.at[0], y_high)
    settle(c0, c1)
    if comm:
        ext_l[:, 2 * OWN : 3 * OWN] = pack(fold_y(recv_y[0], recv_y[1]))
    else:
        ext_l[:, 2 * OWN : 3 * OWN] = jnp.where(lane < 2 * GY, own_l, 0.0)

    def span(step):
        return pl.ds(pl.multiple_of(step * TILE, TILE), TILE)

    def loop(start, stop, step_fn, unroll):
        def one(step, carry):
            step_fn(step)
            return carry

        lax.fori_loop(start, stop, one, 0, unroll=unroll)

    def ahead(start, stop, fetch, use, unroll):
        def one(step, value):
            following = fetch(jnp.minimum(step + 1, stop - 1))
            use(step, value)
            return following

        lax.fori_loop(start, stop, one, fetch(start), unroll=unroll)

    def halves(value):
        return value[:, 0:OWN], value[:, OWN:TILE]

    def get_row(ref, number, step):
        at = number * DENSE + 2 * step
        return jnp.concatenate([ref[pl.ds(at, 1), :], ref[pl.ds(at + 1, 1), :]], axis=1)

    def put_row(ref, number, step, value):
        at = number * DENSE + 2 * step
        low, high = halves(value)
        ref[pl.ds(at, 1), :] = low
        ref[pl.ds(at + 1, 1), :] = high

    def get_eight(ref, step):
        at = 2 * step
        return jnp.concatenate(
            [ref[pl.ds(at, 8, stride=DENSE), :], ref[pl.ds(at + 1, 8, stride=DENSE), :]], axis=1
        )

    def dense(ref, number):
        return ref[number * DENSE : (number + 1) * DENSE, :]

    rel_d[...] = jnp.full_like(rel_d, 2.0)

    def gather_step(step):
        got = mm(ext_l[...], oh2[:, span(step)])
        fb_s[:, span(step)] = got[0:CH]
        relative = unpack(got) - pa_s[:, span(step)]
        for number in range(3):
            put_row(rel_d, number, step, relative[number : number + 1])

    loop(0, STEPS, gather_step, UNROLL_GATHER)

    live = iota((DENSE, OWN), 0) * OWN + iota((DENSE, OWN), 1) < count
    rx = jnp.where(live, dense(rel_d, 0), 2.0)
    ry = jnp.where(live, dense(rel_d, 1), 0.0)
    rz = jnp.where(live, dense(rel_d, 2), 0.0)
    d = jnp.sqrt(rx * rx + ry * ry + rz * rz)
    inv = 1.0 / d
    x, y, z = rx * inv, ry * inv, rz * inv
    scaled = d * (1.0 / CUTOFF)
    left = 1.0 - scaled * scaled
    inside = d < CUTOFF
    values = [
        jnp.full_like(x, SCALE),
        (SCALE * S3) * x,
        (SCALE * S3) * y,
        (SCALE * S3) * z,
        (SCALE * S15) * (x * y),
        (SCALE * S15) * (y * z),
        (SCALE * 0.5 * S5) * (3.0 * z * z - 1.0),
        (SCALE * S15) * (x * z),
        (SCALE * 0.5 * S15) * (x * x - y * y),
        x,
        y,
        z,
        inv,
        jnp.where(inside, left * left, 0.0),
        jnp.where(inside, (-4.0 / CUTOFF) * scaled * left, 0.0),
    ]
    for number, value in enumerate(values):
        geo_d[number * DENSE : (number + 1) * DENSE, :] = value
    sine, cosine = sin_cos(d * (math.pi / CUTOFF))
    twice = 2.0 * cosine
    sine_last, cosine_last = jnp.zeros_like(sine), jnp.ones_like(sine)
    root = math.sqrt(2.0 / CUTOFF)
    for number in range(8):
        bessel = root * sine * inv
        bes_d[number * DENSE : (number + 1) * DENSE, :] = bessel
        slope_d[number * DENSE : (number + 1) * DENSE, :] = (
            (root * (math.pi / CUTOFF) * (number + 1)) * cosine - bessel
        ) * inv
        sine, sine_last = twice * sine - sine_last, sine
        cosine, cosine_last = twice * cosine - cosine_last, cosine

    def network_input(basis):
        a, b, c = split3(basis)
        zero = jnp.zeros_like(a)
        return mm(w6[...], jnp.concatenate([a, b, a, b, c, a, zero, zero], axis=0).astype(BF16))

    def network_output(g):
        hi, lo = split2(g)
        return mm(w3[...], jnp.concatenate([hi, lo, hi], axis=0))

    def radial_fetch(step):
        return network_input(get_eight(bes_d, step))

    def radial_use(step, u):
        hidden = u / (1.0 + jnp.exp(-u))
        r_s[:, span(step)] = network_output(get_row(geo_d, 13, step) * hidden)

    ahead(0, STEPS, radial_fetch, radial_use, UNROLL_RADIAL)

    def slope_fetch(step):
        return network_input(
            jnp.concatenate([get_eight(bes_d, step), get_eight(slope_d, step)], axis=1)
        )

    def slope_use(step, both):
        u, u_d = both[:, :TILE], both[:, TILE:]
        gate = 1.0 / (1.0 + jnp.exp(-u))
        hidden = u * gate
        slope = gate + hidden * (1.0 - gate)
        env, env_d = get_row(geo_d, 13, step), get_row(geo_d, 14, step)
        rp_s[:, span(step)] = network_output(env_d * hidden + env * (slope * u_d))

    def messages(target, step, signs, features, degrees):
        radial = r_s[:, span(step)]
        for degree in degrees:
            product = radial[degree * CH : (degree + 1) * CH] * features
            for q in range(9):
                if DEGREE[q] != degree:
                    continue
                shape = get_row(geo_d, q, step)
                hi, lo = split2((shape * product) if signs[q] > 0 else (-shape * product))
                target[q * CH : (q + 1) * CH, 0:TILE] = hi
                target[q * CH : (q + 1) * CH, TILE : 2 * TILE] = lo

    s2a[...] = jnp.zeros_like(s2a)
    s2b[...] = jnp.zeros_like(s2b)

    def other_step(group):
        degrees, start, stop = GROUPS[group]

        def one(step):
            buffer = m_s.at[lax.rem(step, 2)]
            messages(buffer, step, PARITY, fa_s[:, span(step)], degrees)
            table = oh2[OWN:EXT, span(step)]
            table = jnp.concatenate([table, table], axis=1)
            s2[group][...] += mm(table, buffer[start:stop, :], NT)

        return one

    def push_sums_y(group):
        base = 4 + 2 * group
        src, dst = s2[group], rsy[group]
        return (
            push(base, src.at[pl.ds(OWN, GY)], dst.at[pl.ds(GY, GY)], y_low),
            push(base + 1, src.at[pl.ds(OWN + GY, GY)], dst.at[pl.ds(0, GY)], y_high),
        )

    def push_sums_x(group):
        base = 8 + 2 * group
        src, dst = s2[group], rsx[group]
        return (
            push(base, src.at[pl.ds(0, GX)], dst.at[pl.ds(GX, GX)], x_low),
            push(base + 1, src.at[pl.ds(GX, GX)], dst.at[pl.ds(0, GX)], x_high),
        )

    def add_sums_y(group):
        if comm:
            hi, lo = split2(rsy[group][...])
            table = ohy_t[OWN : 2 * OWN, 0 : 2 * GY]
            s2[group][0:OWN, :] += mm(table, hi) + mm(table, lo)

    s1[...] = jnp.zeros_like(s1)

    def own_sum_step(step):
        messages(m_s.at[0], step, (1.0,) * 9, fb_s[:, span(step)], (0, 1, 2))
        messages(m_s.at[1], step, PARITY, fa_s[:, span(step)], (0, 1, 2))
        table1, table2 = oh1[:, span(step)], oh2[0:OWN, span(step)]
        s1[...] += mm(m_s[0], jnp.concatenate([table1, table1], axis=1), NT) + mm(
            m_s[1], jnp.concatenate([table2, table2], axis=1), NT
        )

    other_step_a, other_step_b = other_step(0), other_step(1)
    loop(0, STEPS, other_step_a, UNROLL_SUMS)
    y_a = push_sums_y(0)
    loop(0, STEPS, other_step_b, UNROLL_SUMS)
    y_b = push_sums_y(1)
    loop(0, 3, own_sum_step, UNROLL_SUMS)
    settle(*y_a)
    add_sums_y(0)
    x_a = push_sums_x(0)
    loop(3, 8, own_sum_step, UNROLL_SUMS)
    settle(*y_b)
    add_sums_y(1)
    x_b = push_sums_x(1)
    loop(8, STEPS, own_sum_step, UNROLL_SUMS)
    ahead(0, STEPS, slope_fetch, slope_use, UNROLL_RADIAL)

    def home_sums(group):
        _, start, stop = GROUPS[group]
        total = s1[start:stop, :]
        if comm:
            hi, lo = split2(rsx[group][...])
            total = total + (home_y[group] + mm(ohx_t, hi) + mm(ohx_t, lo)).T
        return total

    home_y = []
    for group in range(2):
        hi, lo = split2(rsy[group][...])
        table = ohy_t[0:OWN, 0 : 2 * GY]
        home_y.append(mm(table, hi) + mm(table, lo))

    settle(*x_a)
    sums_a = home_sums(0)
    settle(*x_b)
    sums_b = home_sums(1)

    sums = jnp.concatenate([sums_b, sums_a], axis=0)
    squares = [sums[q * CH : (q + 1) * CH] * sums[q * CH : (q + 1) * CH] for q in range(9)]
    invariant = jnp.concatenate(
        [
            squares[0],
            squares[1] + squares[2] + squares[3],
            squares[4] + squares[5] + squares[6] + squares[7] + squares[8],
        ],
        axis=0,
    )
    mixed = mm(mix_ref[...], invariant, precision=HIGHEST) + feat_ref[...].astype(F32)
    gate = 1.0 / (1.0 + jnp.exp(-mixed))
    diagonal = iota((CH, CH), 0) == iota((CH, CH), 1)
    weight = jnp.sum(jnp.where(diagonal, outw_ref[...], 0.0), axis=1, keepdims=True)
    energy = jnp.sum(weight * (mixed * gate), axis=0, keepdims=True)
    kind = spec_ref[...]
    shift = jnp.zeros_like(energy)
    for k in range(5):
        shift = jnp.where(kind == k, se_ref[k], shift)
    energy_ref[...] = energy + shift
    d_mixed = weight * (gate * (1.0 + mixed * (1.0 - gate)))
    d_inv = 2.0 * mm(mix_ref[...].T, d_mixed, precision=HIGHEST)
    gext[...] = jnp.zeros_like(gext)
    for q in range(9):
        at = slice(q * CH, (q + 1) * CH)
        gradient = sums[at] * d_inv[DEGREE[q] * CH : (DEGREE[q] + 1) * CH]
        hi, lo = split2(gradient)
        gown[at, 0:OWN] = hi
        gown[at, OWN : 2 * OWN] = lo
        hi, lo = split2(PARITY[q] * gradient)
        gown2[at, 0:OWN] = hi
        gown2[at, OWN : 2 * OWN] = lo

    def own_rows(table, group):
        _, start, stop = GROUPS[group]
        return mm(table, gown2[start:stop, 0:OWN], NT) + mm(
            table, gown2[start:stop, OWN : 2 * OWN], NT
        )

    def push_gradient_x(group):
        base = 12 + 2 * group
        src, dst = sgx[group], rgx[group]
        src[...] = own_rows(ohx, group)
        return (
            push(base, src.at[pl.ds(0, GX)], dst.at[pl.ds(GX, GX)], x_low),
            push(base + 1, src.at[pl.ds(GX, GX)], dst.at[pl.ds(0, GX)], x_high),
        )

    def push_gradient_y(group, outgoing):
        base = 16 + 2 * group
        src, dst = sgy[group], rgy[group]
        if comm:
            hi, lo = split2(rgx[group][...])
            table = ohy[0 : 2 * GY, OWN : 2 * OWN]
            outgoing = outgoing + mm(table, hi) + mm(table, lo)
        src[...] = outgoing
        return (
            push(base, src.at[pl.ds(0, GY)], dst.at[pl.ds(GY, GY)], y_low),
            push(base + 1, src.at[pl.ds(GY, GY)], dst.at[pl.ds(0, GY)], y_high),
        )

    def store_ghosts(group, ref, start):
        if comm:
            _, first, last = GROUPS[group]
            hi, lo = split2(ref[...].T)
            width = ref.shape[0]
            gext[first:last, start : start + width] = hi
            gext[first:last, 2 * OWN + start : 2 * OWN + start + width] = lo

    x_a = push_gradient_x(0)
    x_b = push_gradient_x(1)
    outgoing_a = own_rows(ohy[0 : 2 * GY, 0:OWN], 0)
    outgoing_b = own_rows(ohy[0 : 2 * GY, 0:OWN], 1)

    def contract(step, terms, first_row, target, degrees, last):
        along = None
        for degree in degrees:
            part = slice(degree * CH, (degree + 1) * CH)
            radial, slope = r_s[part, span(step)], rp_s[part, span(step)]
            total = None
            for q in range(9):
                if DEGREE[q] != degree:
                    continue
                rows = slice(q * CH - first_row, (q + 1) * CH - first_row)
                here = None
                for gathered, features in terms:
                    product = gathered[rows] * features
                    here = product if here is None else here + product
                put_row(target, q, step, jnp.sum(radial * here, axis=0, keepdims=True))
                term = get_row(geo_d, q, step) * here
                total = term if total is None else total + term
            along = slope * total if along is None else along + slope * total
        put_row(target, last, step, jnp.sum(along, axis=0, keepdims=True))

    def own_step(step):
        table1, table2 = oh1[:, span(step)], oh2[0:OWN, span(step)]
        first = mm(gown[...], jnp.concatenate([table1, table1], axis=0))
        second = mm(gown2[...], jnp.concatenate([table2, table2], axis=0))
        terms = ((first, fb_s[:, span(step)]), (second, fa_s[:, span(step)]))
        contract(step, terms, 0, z_own, (0, 1, 2), 9)

    loop(0, STEPS, own_step, UNROLL_BACK)
    settle(*x_a)
    y_a = push_gradient_y(0, outgoing_a)
    store_ghosts(0, rgxa, 0)
    settle(*x_b)
    y_b = push_gradient_y(1, outgoing_b)
    store_ghosts(1, rgxb, 0)

    def ext_step(group):
        degrees, first, last = GROUPS[group]

        def fetch(step):
            table = oh2[OWN:EXT_PAD, span(step)]
            return mm(gext[first:last, :], jnp.concatenate([table, table], axis=0))

        def use(step, gathered):
            terms = ((gathered, fa_s[:, span(step)]),)
            contract(step, terms, first, z_ext, degrees, 9 + group)

        return fetch, use

    ext_a, ext_b = ext_step(0), ext_step(1)
    settle(*y_a)
    store_ghosts(0, rgya, OWN)
    ahead(0, STEPS, *ext_a, UNROLL_BACK)
    settle(*y_b)
    store_ghosts(1, rgyb, OWN)
    ahead(0, STEPS, *ext_b, UNROLL_BACK)

    zs = [dense(z_own, q) + dense(z_ext, q) for q in range(10)]
    zs[9] = zs[9] + dense(z_ext, 10)
    nx, ny, nz, inv = [dense(geo_d, number) for number in range(9, 13)]
    factor = SCALE * inv
    gx = factor * (S3 * zs[1] + S15 * (ny * zs[4] + nz * zs[7] + nx * zs[8]))
    gy = factor * (S3 * zs[2] + S15 * (nx * zs[4] + nz * zs[5] - ny * zs[8]))
    gz = factor * (S3 * zs[3] + S15 * (ny * zs[5] + nx * zs[7]) + (3.0 * S5) * (nz * zs[6]))
    along = zs[9] - (gx * nx + gy * ny + gz * nz)
    pull_d[...] = jnp.zeros_like(pull_d)
    for number, value in enumerate([gx + along * nx, gy + along * ny, gz + along * nz]):
        pull_d[number * DENSE : (number + 1) * DENSE, :] = value
    for step in range(STEPS):
        pulled = get_eight(pull_d, step)
        hi = pulled.astype(BF16).astype(F32)
        pieces_s[:, step * TILE : (step + 1) * TILE] = jnp.concatenate(
            [hi, pulled - hi], axis=0
        ).astype(BF16)
    at_first = mm(oh1[...], pieces_s[...], NT)
    at_second = mm(oh2[...], pieces_s[...], NT)

    def home(rows8, table):
        a, b, c = split3(rows8)
        out = mm(jnp.concatenate([a, b, c, jnp.zeros_like(a)], axis=0).astype(BF16), table)
        return out[0:8] + out[8:16] + out[16:24]

    at_first, at_second = at_first.T, -at_second.T
    at_first = at_first[0:8] + at_first[8:16]
    total = at_second[0:8] + at_second[8:16]
    send_f[0] = total[:, 2 * OWN : 3 * OWN]
    c0 = push(20, send_f.at[0], recv_f.at[1], y_low)
    c1 = push(21, send_f.at[0], recv_f.at[0], y_high)
    settle(c0, c1)
    near = jnp.concatenate([total[:, 0:OWN] + at_first, total[:, OWN : 2 * OWN]], axis=1)
    if comm:
        near = near + home(fold_y(recv_f[0], recv_f[1]), ohy)
    send_f[1] = near[:, OWN : 2 * OWN]
    c0 = push(22, send_f.at[1], recv_f.at[3], x_low)
    c1 = push(23, send_f.at[1], recv_f.at[2], x_high)
    settle(c0, c1)
    own = near[:, 0:OWN]
    if comm:
        own = own + home(fold_x(recv_f[2], recv_f[3]), ohx)
    force_ref[...] = own[0:3]


def run(args, n_gx, n_gy, comm=True):
    (
        positions,
        features,
        species,
        edge_list,
        edge_count,
        send_list_x,
        send_list_y,
        radial_in,
        radial_out,
        mix_weight,
        out_weight,
        species_energy,
    ) = args
    vmem = pl.BlockSpec(memory_space=pltpu.VMEM)
    smem = pl.BlockSpec(memory_space=pltpu.SMEM)
    scratch = [
        pltpu.VMEM((8, OWN), F32),
        pltpu.VMEM((1, OWN), jnp.int32),
        pltpu.VMEM((OWN, SLOTS), BF16),
        pltpu.VMEM((EXT_PAD, SLOTS), BF16),
        pltpu.VMEM((2, CH // 2 + 8, OWN), F32),
        pltpu.VMEM((2, CH // 2 + 8, OWN), F32),
        pltpu.VMEM((CH + 8, OWN), F32),
        pltpu.VMEM((2, CH + 8, OWN), F32),
        pltpu.VMEM((CH + 32, EXT_PAD), BF16),
        pltpu.VMEM((8, SLOTS), F32),
        pltpu.VMEM((3 * DENSE, OWN), F32),
        pltpu.VMEM((8 * DENSE, OWN), F32),
        pltpu.VMEM((8 * DENSE, OWN), F32),
        pltpu.VMEM((16 * DENSE, OWN), F32),
        pltpu.VMEM((8 * DENSE, OWN), F32),
        pltpu.VMEM((CH, SLOTS), F32),
        pltpu.VMEM((CH, SLOTS), F32),
        pltpu.VMEM((3 * CH, SLOTS), F32),
        pltpu.VMEM((3 * CH, SLOTS), F32),
        pltpu.VMEM((3 * CH, 3 * CH), BF16),
        pltpu.VMEM((CH, 64), BF16),
        pltpu.VMEM((2, ROWS, 2 * TILE), BF16),
        pltpu.VMEM((ROWS, OWN), F32),
        pltpu.VMEM((EXT - OWN, 5 * CH), F32),
        pltpu.VMEM((EXT - OWN, 4 * CH), F32),
        pltpu.VMEM((2 * GY, 5 * CH), F32),
        pltpu.VMEM((2 * GY, 4 * CH), F32),
        pltpu.VMEM((2 * GX, 5 * CH), F32),
        pltpu.VMEM((2 * GX, 4 * CH), F32),
        pltpu.VMEM((ROWS, 2 * OWN), BF16),
        pltpu.VMEM((ROWS, 2 * OWN), BF16),
        pltpu.VMEM((ROWS, 4 * OWN), BF16),
        pltpu.VMEM((2 * GX, 5 * CH), F32),
        pltpu.VMEM((2 * GX, 4 * CH), F32),
        pltpu.VMEM((2 * GX, 5 * CH), F32),
        pltpu.VMEM((2 * GX, 4 * CH), F32),
        pltpu.VMEM((2 * GY, 5 * CH), F32),
        pltpu.VMEM((2 * GY, 4 * CH), F32),
        pltpu.VMEM((2 * GY, 5 * CH), F32),
        pltpu.VMEM((2 * GY, 4 * CH), F32),
        pltpu.VMEM((10 * DENSE, OWN), F32),
        pltpu.VMEM((11 * DENSE, OWN), F32),
        pltpu.VMEM((16, SLOTS), BF16),
        pltpu.VMEM((2, 8, OWN), F32),
        pltpu.VMEM((4, 8, OWN), F32),
        pltpu.SemaphoreType.DMA((24,)),
        pltpu.SemaphoreType.DMA((24,)),
    ]
    params = {"collective_id": 0, "has_side_effects": True} if comm else {}
    energies, forces = pl.pallas_call(
        functools.partial(body, comm, n_gx, n_gy),
        out_shape=(
            jax.ShapeDtypeStruct((1, OWN), F32),
            jax.ShapeDtypeStruct((3, OWN), F32),
        ),
        in_specs=[vmem, vmem, vmem, vmem, smem, vmem, vmem, vmem, vmem, vmem, vmem, smem],
        out_specs=(vmem, vmem),
        scratch_shapes=scratch,
        compiler_params=pltpu.CompilerParams(vmem_limit_bytes=60 * 1024 * 1024, **params),
        name="layer",
    )(
        positions,
        features,
        species.reshape(1, -1),
        edge_list,
        edge_count,
        send_list_x.reshape(1, -1),
        send_list_y.reshape(1, -1),
        radial_in.T,
        radial_out.T,
        mix_weight,
        out_weight.reshape(1, -1),
        species_energy,
    )
    return energies.reshape(-1), forces


def solution(mesh):
    n_gx, n_gy = mesh.shape["gx"], mesh.shape["gy"]
    both = ("gx", "gy")
    placed = (
        P(None, both),
        P(None, both),
        P(both),
        P(None, both),
        P(both),
        P(both),
        P(both),
        P(),
        P(),
        P(),
        P(),
        P(),
    )
    return jax.shard_map(
        lambda *args: run(args, n_gx, n_gy),
        mesh=mesh,
        in_specs=placed,
        out_specs=(P(both), P(None, both)),
        check_vma=False,
    )
```
